256 devices in a mesh: task: 8 (over z_hi, core), row: 8 (over x, z_lo), col: 4 (over y).
Axes of the slice: x: 4, y: 4, z: 8 (z_hi: 4, z_lo: 2; z = z_hi * 2 + z_lo), core: 2. Of those that a mesh axis runs over, the one named last changes fastest.
Arguments:
- activations: bfloat16 [8, 512, 13824], P('task', 'col', 'row'), may hold values from -6 to 6
- weights: bfloat16 [8, 13824, 5120], P('task', 'row', 'col'), may hold values from -0.0625 to 0.0625
- labels: int32 [8, 512], P('task'), may hold values from 0 to 127
- prototypes: bfloat16 [8, 128, 5120], P('task', None, 'col'), may hold values from -6 to 6
Outputs:
- merged: bfloat16 [13824, 5120], P('row', 'col')
- merged_out: bfloat16 [8, 512, 5120], P('task', 'row', 'col')
The draws below stay inside these ranges and needn't reach their ends.
All inputs are finite; a program needn't handle non-finite values.
Results may differ from the reference program's by a relative error of at most 0.02.
Values may be sent and summed in bfloat16 or wider, within the bound.
A program may use at most 128 MiB of HBM per device.

```python
import jax
import jax.numpy as jnp
from jax import lax

D = 5120
FF = 13824
CLASSES = 128
TOK = 512
TASKS = 8


def plant(array, own_key, least, high):
    longest = array.shape.index(max(array.shape))
    spots = []
    for shift in (0, 1):
        where = [jax.random.randint(jax.random.fold_in(own_key, axis), (), 0, length) for axis, length in enumerate(array.shape)]
        where[longest] = (where[longest] + shift) % array.shape[longest]
        spots.append(tuple(where))
    return array.at[spots[0]].set(least).at[spots[1]].set(high)


def strengthened(values, own_key, source, target, blocks, factor):
    def block_of(position):
        return (jnp.arange(values.shape[position]) // (values.shape[position] // blocks)).reshape((-1,) + (1,) * (values.ndim - 1 - position))

    near = jax.random.permutation(own_key, blocks)[block_of(target)]
    second = (block_of(target) + blocks // 2) % blocks
    return jnp.where((block_of(source) == near) | (block_of(source) == second), factor * values, values)


def steps_of(stream_key, extent, shards, smallest, high):
    def one(position, parts):
        steps = jax.random.uniform(jax.random.fold_in(jax.random.fold_in(stream_key, 6), position), (parts,), jnp.float32, smallest / len(shards), high / len(shards))
        return jnp.repeat(jnp.exp(steps), extent[position] // parts).reshape((-1,) + (1,) * (len(extent) - position - 1))

    loudness = one(*shards[0])
    for cut in shards[1:]:
        loudness = loudness * one(*cut)
    return loudness


def noise(own_key, extent, deviation, reach, pieces=(), kind=jnp.bfloat16):
    gain = steps_of(own_key, extent, pieces, -0.22, 0.18) if pieces else 1.0
    drawn = jax.random.normal(own_key, extent, jnp.float32) * deviation * gain
    return jnp.minimum(jnp.maximum(drawn, -reach), reach).astype(kind)


def gaussian_with(key, extent, spread, reach, split, heavy, kind=jnp.bfloat16):
    values = spread * jax.random.normal(key, extent, jnp.float32)
    if split:
        values = values * steps_of(key, extent, split, -0.22, 0.18)
    return jnp.clip(strengthened(values, jax.random.fold_in(key, 3), *heavy), -reach, reach).astype(kind)


def setup_inputs(seed: int = 0) -> dict:
    arg_keys = jax.random.split(jax.random.key(seed), 5)
    return {
        "activations": noise(arg_keys[0], (TASKS, TOK, FF), 1.0, 6.0, ((0, 8), (1, 4), (2, 8))),
        "weights": gaussian_with(arg_keys[1], (TASKS, FF, D), FF ** -0.5, 0.0625, ((0, 8), (1, 8), (2, 4)), (0, 1, 8, 2.0)),
        "labels": plant(jax.random.randint(arg_keys[2], (TASKS, TOK), 0, CLASSES), jax.random.fold_in(arg_keys[2], 1), 0, CLASSES - 1).astype(jnp.int32),
        "prototypes": noise(arg_keys[3], (TASKS, CLASSES, D), 1.0, 6.0, ((0, 8), (2, 4))),
    }


def reference(activations, weights, labels, prototypes):
    def accumulate(carry, items):
        acts, weight, label_row, protos = items
        output = jnp.dot(acts, weight, preferred_element_type=jnp.float32)
        onehot = (label_row[:, None] == jnp.arange(CLASSES, dtype=jnp.int32)[None, :]).astype(jnp.bfloat16)
        target = jnp.dot(onehot, protos, preferred_element_type=jnp.float32)
        grad = output - target
        gsq = (grad * grad).astype(jnp.bfloat16)
        wide = acts.astype(jnp.float32)
        asq = (wide * wide).astype(jnp.bfloat16)
        fisher = jnp.dot(asq.T, gsq, preferred_element_type=jnp.float32)
        numer, denom = carry
        return (numer + fisher * weight.astype(jnp.float32), denom + fisher), None

    start = (jnp.zeros((FF, D), jnp.float32), jnp.zeros((FF, D), jnp.float32))
    (numer, denom), _ = lax.scan(accumulate, start, (activations, weights, labels, prototypes))
    merged = (numer / (denom + 1e-6)).astype(jnp.bfloat16)
    merged_out = lax.map(lambda acts: jnp.dot(acts, merged, preferred_element_type=jnp.float32).astype(jnp.bfloat16), activations)
    return merged, merged_out
```

```python
import functools

import jax
import jax.numpy as jnp
from jax import lax
from jax.experimental import pallas as pl
from jax.experimental.pallas import tpu as pltpu
from jax.sharding import PartitionSpec as P

MESH = pl.DeviceIdType.MESH
F32, BF16 = jnp.float32, jnp.bfloat16
ZH, XS, YS = 4, 4, 4
CW = 256
HALF = CW // 2

X1, Z1, Z2, X2, CORE, FAR, NEAR, SUM, MERGED, FORWARD, SHARE, X3, Z3 = 0, 3, 4, 5, 8, 9, 11, 13, 15, 17, 18, 22, 25
SLOTS = 26


def kernel(
    chunks, acts_in, w_in, labels, protos, merged_out, out,
    acts, w, asq_t, target, part, part_in, row_sum, z_send, z_in, gsq, nd, nd_in, nd_sum,
    far_in, near_in, sum_in, merged, part2, part2_in, row_sum2, z_send2, z_in2,
    send_sem, recv_sem, gather_send, gather_recv, local_sem, store_sem,
):
    task, row, y = lax.axis_index("task"), lax.axis_index("row"), lax.axis_index("col")
    zh, core = task // 2, task % 2
    x, zl = row // 2, row % 2
    tok, units = acts.shape
    block = tok // XS
    half = block // 2
    piece = units // ZH

    def at_x(step):
        return {"row": (x + step) % XS * 2 + zl}

    pair = {"row": x * 2 + 1 - zl}
    twin = {"task": zh * 2 + 1 - core}

    def at_z(step):
        return {"task": (zh + step + ZH) % ZH * 2 + core}

    def at_y(step):
        return {"col": (y + step + YS) % YS}

    def rows_of(index, size):
        return pl.ds(pl.multiple_of(index * size, size), size)

    def z_piece(step):
        return rows_of((zh + step + ZH) % ZH, piece)

    mine = pl.ds(pl.multiple_of(core * HALF, HALF), HALF)
    others = pl.ds(pl.multiple_of((1 - core) * HALF, HALF), HALF)

    def remote(src, dst, c, slot, device):
        return pltpu.make_async_remote_copy(
            src_ref=src, dst_ref=dst, send_sem=send_sem.at[c, slot], recv_sem=recv_sem.at[c, slot],
            device_id=device, device_id_type=MESH,
        )

    def x1(c, d):
        return remote(part.at[c, rows_of((x + d) % XS, block)], part_in.at[c, d - 1], c, X1 + d - 1, at_x(d))

    def z1(c):
        return remote(z_send.at[c], z_in.at[c], c, Z1, pair)

    def z2(c):
        here = gsq.at[c, rows_of(row, half)]
        return remote(here, here, c, Z2, pair)

    def x2(c, d):
        here = gsq.at[c, rows_of(x, block)]
        return remote(here, here, c, X2 + d - 1, at_x(d))

    def across(c):
        return remote(nd.at[c, :, :, others], nd_in.at[c], c, CORE, twin)

    def far(c, k):
        return remote(nd_sum.at[c, k, z_piece(2)], far_in.at[c, k], c, FAR + k, at_z(1 - 2 * k))

    def near(c, k):
        return remote(nd_sum.at[c, 1 - k, z_piece(1 - 2 * k)], near_in.at[c, k], c, NEAR + k, at_z(1 - 2 * k))

    def summed(c, k):
        return remote(nd_sum.at[c, k, z_piece(1 - 2 * k)], sum_in.at[c, k], c, SUM + k, at_z(1 - 2 * k))

    def spread(c, k):
        here = merged.at[c, z_piece(0), mine]
        return remote(here, here, c, MERGED + k, at_z(1 - 2 * k))

    def forward(c):
        here = merged.at[c, z_piece(2 * core - 1), mine]
        return remote(here, here, c, FORWARD, at_z(1 - 2 * core))

    def share(c, step):
        here = merged.at[c, z_piece(step), mine]
        return remote(here, here, c, SHARE + step, twin)

    def x3(c, d):
        return remote(part2.at[c, rows_of((x + d) % XS, block)], part2_in.at[c, d - 1], c, X3 + d - 1, at_x(d))

    def z3(c):
        return remote(z_send2.at[c], z_in2.at[c], c, Z3, pair)

    def store(c):
        return pltpu.make_async_copy(
            merged.at[c], merged_out.at[:, pl.ds(pl.multiple_of(c * CW, CW), CW)], store_sem.at[c]
        )

    own = rows_of(y, block)
    load_acts = pltpu.make_async_copy(acts_in, acts.at[own], local_sem.at[chunks])
    load_acts.start()
    loads = [
        pltpu.make_async_copy(w_in.at[:, pl.ds(c * CW, CW)], w.at[c], local_sem.at[c]) for c in range(chunks)
    ]
    for load in loads:
        load.start()

    barrier = pltpu.get_barrier_semaphore()
    peers = [at_y(1), at_y(-1), at_x(1), at_x(2), at_x(3), pair, twin, at_z(1), at_z(-1)]
    for peer in peers:
        pl.semaphore_signal(barrier, inc=1, device_id=peer, device_id_type=MESH)
    pl.semaphore_wait(barrier, len(peers))

    def gather(src, index, slot, device):
        return pltpu.make_async_remote_copy(
            src_ref=src, dst_ref=acts.at[rows_of(index, block)], send_sem=gather_send.at[slot],
            recv_sem=gather_recv.at[slot], device_id=device, device_id_type=MESH,
        )

    up, down = gather(acts_in, y, 0, at_y(1)), gather(acts_in, y, 1, at_y(-1))
    up.start()
    down.start()

    onehot = (
        labels[rows_of(row, half), :] == lax.broadcasted_iota(jnp.int32, (half, protos.shape[0]), 1)
    ).astype(F32).astype(BF16)
    target[...] = jnp.dot(onehot, protos[...], preferred_element_type=F32)

    def square(index):
        wide = acts[rows_of(index, block), :].astype(F32)
        asq_t[:, rows_of(index, block)] = (wide * wide).T.astype(BF16)

    load_acts.wait()
    square(y)
    up.wait_recv()
    down.wait_recv()
    source = (y + 2 * core - 1 + YS) % YS
    onward = gather(acts.at[rows_of(source, block)], source, 2, at_y(1 - 2 * core))
    onward.start()
    square((y + 1) % YS)
    square((y + 3) % YS)
    onward.wait_recv()
    square((y + 2) % YS)
    for load in loads:
        load.wait()

    def product(left, c, right, result):
        for m in range(2):
            rows = pl.ds(m * (tok // 2), tok // 2)
            result[c, rows, :] = jnp.dot(left[rows, :], right[c], preferred_element_type=F32).astype(BF16)

    def reduce_x(c, own_part, arrived, start):
        rows = pl.ds(pl.multiple_of(start, half), half)
        total = own_part[c, pl.ds(pl.multiple_of(x * block + start, half), half), :].astype(F32)
        for d in range(XS - 1):
            total = total + arrived[c, d, rows, :].astype(F32)
        return total

    def s1(c):
        product(acts, c, w, part)
        for d in (1, 2, 3):
            x1(c, d).start()

    def s2(c):
        for d in (1, 2, 3):
            x1(c, d).wait_recv()
        z_send[c] = reduce_x(c, part, part_in, (1 - zl) * half).astype(BF16)
        z1(c).start()
        row_sum[c] = reduce_x(c, part, part_in, zl * half)

    def s3(c):
        z1(c).wait_recv()
        grad = row_sum[c] + z_in[c].astype(F32) - target[:, pl.ds(pl.multiple_of(c * CW, CW), CW)]
        gsq[c, rows_of(row, half), :] = (grad * grad).astype(BF16)
        z2(c).start()

    def s4(c):
        z2(c).wait_recv()
        for d in (1, 2, 3):
            x2(c, d).start()

    def s5(c):
        for d in (1, 2, 3):
            x2(c, d).wait_recv()
        for q in range(ZH):
            rows = pl.ds(q * piece, piece)
            fisher = jnp.dot(asq_t[rows, :], gsq[c], preferred_element_type=F32)
            nd[c, 0, rows, :] = (fisher * w[c, rows, :].astype(F32)).astype(BF16)
            nd[c, 1, rows, :] = fisher.astype(BF16)
        across(c).start()

    def s6(c):
        across(c).wait_recv()

        def add(k, step):
            rows = z_piece(step)
            nd_sum[c, k, rows, :] = (nd[c, k, rows, mine].astype(F32) + nd_in[c, k, rows, :].astype(F32)).astype(BF16)

        add(0, 2)
        far(c, 0).start()
        add(1, 2)
        far(c, 1).start()
        add(1, 1)
        near(c, 0).start()
        add(0, -1)
        near(c, 1).start()
        add(0, 1)
        add(1, -1)
        add(0, 0)
        add(1, 0)

    def s7(c):
        for k in range(2):
            far(c, k).wait_recv()
            rows = z_piece(1 - 2 * k)
            nd_sum[c, k, rows, :] = (nd_sum[c, k, rows, :].astype(F32) + far_in[c, k].astype(F32)).astype(BF16)
            summed(c, k).start()

    def s8(c):
        for k in range(2):
            near(c, k).wait_recv()
            summed(c, k).wait_recv()
        rows = z_piece(0)
        numer = nd_sum[c, 0, rows, :].astype(F32) + near_in[c, 1].astype(F32) + sum_in[c, 0].astype(F32)
        denom = nd_sum[c, 1, rows, :].astype(F32) + near_in[c, 0].astype(F32) + sum_in[c, 1].astype(F32)
        merged[c, rows, mine] = (numer / (denom + 1e-6)).astype(BF16)
        spread(c, 0).start()
        spread(c, 1).start()
        share(c, 0).start()

    def s9(c):
        spread(c, 0).wait_recv()
        spread(c, 1).wait_recv()
        forward(c).start()
        share(c, 1).start()
        share(c, 3).start()

    def s10(c):
        forward(c).wait_recv()
        share(c, 2).start()

    def s11(c):
        for step in range(ZH):
            share(c, step).wait_recv()
        product(acts, c, merged, part2)
        for d in (1, 2, 3):
            x3(c, d).start()
        store(c).start()

    def s12(c):
        for d in (1, 2, 3):
            x3(c, d).wait_recv()
        z_send2[c] = reduce_x(c, part2, part2_in, (1 - zl) * half).astype(BF16)
        z3(c).start()
        row_sum2[c] = reduce_x(c, part2, part2_in, zl * half)

    def s13(c):
        z3(c).wait_recv()
        out[:, pl.ds(pl.multiple_of(c * CW, CW), CW)] = (row_sum2[c] + z_in2[c].astype(F32)).astype(BF16)

    stages = [s1, s2, s3, s4, s5, s6, s7, s8, s9, s10, s11, s12, s13]

    @pl.loop(0, chunks + len(stages) - 1)
    def _(tick):
        for k in reversed(range(len(stages))):
            c = tick - k

            @pl.when((c >= 0) & (c < chunks))
            def _():
                stages[k](c)

    up.wait_send()
    down.wait_send()
    onward.wait_send()

    @pl.loop(0, chunks)
    def _(c):
        for d in (1, 2, 3):
            x1(c, d).wait_send()
            x2(c, d).wait_send()
            x3(c, d).wait_send()
        for copy in (z1, z2, z3, across, forward):
            copy(c).wait_send()
        for k in range(2):
            for copy in (far, near, summed, spread):
                copy(c, k).wait_send()
        for step in range(ZH):
            share(c, step).wait_send()
        store(c).wait()


def local(activations, weights, labels, prototypes):
    shard, units = activations.shape[1:]
    tok, wide = labels.shape[1], weights.shape[2]
    chunks, block, half, piece = wide // CW, tok // XS, tok // XS // 2, units // ZH

    def vmem(*shape, kind=BF16):
        return pltpu.VMEM(shape, kind)

    anywhere = pl.BlockSpec(memory_space=pl.ANY)
    inside = pl.BlockSpec(memory_space=pltpu.VMEM)
    merged, result = pl.pallas_call(
        functools.partial(kernel, chunks),
        out_shape=(
            jax.ShapeDtypeStruct((units, wide), BF16),
            jax.ShapeDtypeStruct((half, wide), BF16),
        ),
        in_specs=[anywhere, anywhere, inside, inside],
        out_specs=(anywhere, inside),
        scratch_shapes=[
            vmem(tok, units),
            vmem(chunks, units, CW),
            vmem(units, tok),
            vmem(half, wide, kind=F32),
            vmem(chunks, tok, CW),
            vmem(chunks, XS - 1, block, CW),
            vmem(chunks, half, CW, kind=F32),
            vmem(chunks, half, CW),
            vmem(chunks, half, CW),
            vmem(chunks, tok, CW),
            vmem(chunks, 2, units, CW),
            vmem(chunks, 2, units, HALF),
            vmem(chunks, 2, units, HALF),
            vmem(chunks, 2, piece, HALF),
            vmem(chunks, 2, piece, HALF),
            vmem(chunks, 2, piece, HALF),
            vmem(chunks, units, CW),
            vmem(chunks, tok, CW),
            vmem(chunks, XS - 1, block, CW),
            vmem(chunks, half, CW, kind=F32),
            vmem(chunks, half, CW),
            vmem(chunks, half, CW),
            pltpu.SemaphoreType.DMA((chunks, SLOTS)),
            pltpu.SemaphoreType.DMA((chunks, SLOTS)),
            pltpu.SemaphoreType.DMA((3,)),
            pltpu.SemaphoreType.DMA((3,)),
            pltpu.SemaphoreType.DMA((chunks + 1,)),
            pltpu.SemaphoreType.DMA((chunks,)),
        ],
        compiler_params=pltpu.CompilerParams(
            collective_id=0, has_side_effects=True, vmem_limit_bytes=60 << 20
        ),
    )(activations[0], weights[0], labels.reshape(tok, 1), prototypes[0])
    return merged, result[None]


def solution(mesh):
    placed = (
        P("task", "col", "row"),
        P("task", "row", "col"),
        P("task", None),
        P("task", None, "col"),
    )
    return jax.shard_map(
        local,
        mesh=mesh,
        in_specs=placed,
        out_specs=(P("row", "col"), P("task", "row", "col")),
        check_vma=False,
    )
```

```python
import functools

import jax
import jax.numpy as jnp
from jax import lax
from jax.experimental import pallas as pl
from jax.experimental.pallas import tpu as pltpu
from jax.sharding import PartitionSpec as P

MESH = pl.DeviceIdType.MESH
F32, BF16 = jnp.float32, jnp.bfloat16
ZH, XS, YS = 4, 4, 4
CW = 256
HALF = CW // 2

X1, Z1, Z2, X2, CORE, FAR, NEAR, SUM, MERGED, FORWARD, SHARE, X3, Z3 = 0, 3, 4, 5, 8, 9, 11, 13, 15, 17, 18, 22, 25
SLOTS = 26


def kernel(
    chunks, acts_in, w_in, labels_in, protos_in, merged_out, out,
    labels, protos, acts_t, acts, w, asq_t, target, part, part_in, row_sum, z_send, z_in, gsq, nd, nd_in, nd_sum,
    far_in, near_in, sum_in, merged, part2, part2_in, row_sum2, z_send2, z_in2,
    send_sem, recv_sem, gather_send, gather_recv, local_sem, store_sem,
):
    task, row, y = lax.axis_index("task"), lax.axis_index("row"), lax.axis_index("col")
    zh, core = task // 2, task % 2
    x, zl = row // 2, row % 2
    tok, units = acts.shape
    block = tok // XS
    half = block // 2
    piece = units // ZH

    def at_x(step):
        return {"row": (x + step) % XS * 2 + zl}

    pair = {"row": x * 2 + 1 - zl}
    twin = {"task": zh * 2 + 1 - core}

    def at_z(step):
        return {"task": (zh + step + ZH) % ZH * 2 + core}

    def at_y(step):
        return {"col": (y + step + YS) % YS}

    def rows_of(index, size):
        return pl.ds(pl.multiple_of(index * size, size), size)

    def z_piece(step):
        return rows_of((zh + step + ZH) % ZH, piece)

    mine = pl.ds(pl.multiple_of(core * HALF, HALF), HALF)
    others = pl.ds(pl.multiple_of((1 - core) * HALF, HALF), HALF)

    def remote(src, dst, c, slot, device):
        return pltpu.make_async_remote_copy(
            src_ref=src, dst_ref=dst, send_sem=send_sem.at[c, slot], recv_sem=recv_sem.at[c, slot],
            device_id=device, device_id_type=MESH,
        )

    def x1(c, d):
        return remote(part.at[c, rows_of((x + d) % XS, block)], part_in.at[c, d - 1], c, X1 + d - 1, at_x(d))

    def z1(c):
        return remote(z_send.at[c], z_in.at[c], c, Z1, pair)

    def z2(c):
        here = gsq.at[c, rows_of(row, half)]
        return remote(here, here, c, Z2, pair)

    def x2(c, d):
        here = gsq.at[c, rows_of(x, block)]
        return remote(here, here, c, X2 + d - 1, at_x(d))

    def across(c):
        return remote(nd.at[c, :, :, others], nd_in.at[c], c, CORE, twin)

    def far(c, k):
        return remote(nd_sum.at[c, k, z_piece(2)], far_in.at[c, k], c, FAR + k, at_z(1 - 2 * k))

    def near(c, k):
        return remote(nd_sum.at[c, 1 - k, z_piece(1 - 2 * k)], near_in.at[c, k], c, NEAR + k, at_z(1 - 2 * k))

    def summed(c, k):
        return remote(nd_sum.at[c, k, z_piece(1 - 2 * k)], sum_in.at[c, k], c, SUM + k, at_z(1 - 2 * k))

    def spread(c, k):
        here = merged.at[c, z_piece(0), mine]
        return remote(here, here, c, MERGED + k, at_z(1 - 2 * k))

    def forward(c):
        here = merged.at[c, z_piece(2 * core - 1), mine]
        return remote(here, here, c, FORWARD, at_z(1 - 2 * core))

    def share(c, step):
        here = merged.at[c, z_piece(step), mine]
        return remote(here, here, c, SHARE + step, twin)

    def x3(c, d):
        return remote(part2.at[c, rows_of((x + d) % XS, block)], part2_in.at[c, d - 1], c, X3 + d - 1, at_x(d))

    def z3(c):
        return remote(z_send2.at[c], z_in2.at[c], c, Z3, pair)

    def store(c):
        return pltpu.make_async_copy(
            merged.at[c], merged_out.at[:, pl.ds(pl.multiple_of(c * CW, CW), CW)], store_sem.at[c]
        )

    load_acts = pltpu.make_async_copy(acts_in, acts_t.at[y], local_sem.at[chunks])
    load_acts.start()
    loads = [
        pltpu.make_async_copy(w_in.at[:, pl.ds(c * CW, CW)], w.at[c], local_sem.at[c]) for c in range(chunks)
    ]
    for load in loads:
        load.start()
    small = [
        pltpu.make_async_copy(labels_in, labels, local_sem.at[chunks + 1]),
        pltpu.make_async_copy(protos_in, protos, local_sem.at[chunks + 2]),
    ]
    for load in small:
        load.start()

    barrier = pltpu.get_barrier_semaphore()
    peers = [at_y(1), at_y(-1), at_x(1), at_x(2), at_x(3), pair, twin, at_z(1), at_z(-1)]
    for peer in peers:
        pl.semaphore_signal(barrier, inc=1, device_id=peer, device_id_type=MESH)
    pl.semaphore_wait(barrier, len(peers))

    pieces = [pl.ds(0, units // 2), pl.ds(units // 2, units // 2)]

    def gather(src, index, slot, h, device):
        return pltpu.make_async_remote_copy(
            src_ref=src.at[pieces[h]], dst_ref=acts_t.at[index, pieces[h]], send_sem=gather_send.at[slot, h],
            recv_sem=gather_recv.at[slot, h], device_id=device, device_id_type=MESH,
        )

    up = [gather(acts_in, y, 0, h, at_y(1)) for h in range(2)]
    down = [gather(acts_in, y, 1, h, at_y(-1)) for h in range(2)]
    source = (y + 2 * core - 1 + YS) % YS
    onward = [gather(acts_t.at[source], source, 2, h, at_y(1 - 2 * core)) for h in range(2)]
    for h in range(2):
        up[h].start()
        down[h].start()

    def tokens(index):
        rows = rows_of(index, block)
        turned = acts_t[index]
        acts[rows, :] = turned.T
        wide = turned.astype(F32)
        asq_t[:, rows] = (wide * wide).astype(BF16)
        step = (index - x + XS) % XS

        @pl.loop(0, chunks)
        def _(c):
            part[c, rows, :] = jnp.dot(acts[rows, :], w[c], preferred_element_type=F32).astype(BF16)

            @pl.when(step != 0)
            def _():
                x1(c, step).start()

    for load in small:
        load.wait()
    onehot = (
        labels[:, rows_of(x, block)] == lax.broadcasted_iota(jnp.int32, (protos.shape[0], block), 0)
    ).astype(F32).astype(BF16)
    target[...] = lax.dot_general(onehot, protos[...], (((0,), (0,)), ((), ())), preferred_element_type=F32)

    load_acts.wait()
    for load in loads:
        load.wait()
    tokens(y)
    for h in range(2):
        up[h].wait_recv()
        down[h].wait_recv()
        onward[h].start()
    tokens((y + 1) % YS)
    tokens((y + 3) % YS)
    for h in range(2):
        onward[h].wait_recv()
    tokens((y + 2) % YS)

    def product(left, c, right, result):
        for m in range(2):
            rows = pl.ds(m * (tok // 2), tok // 2)
            result[c, rows, :] = jnp.dot(left[rows, :], right[c], preferred_element_type=F32).astype(BF16)

    def reduce_x(c, own_part, arrived, start):
        rows = pl.ds(pl.multiple_of(start, half), half)
        total = own_part[c, pl.ds(pl.multiple_of(x * block + start, half), half), :].astype(F32)
        for d in range(XS - 1):
            total = total + arrived[c, d, rows, :].astype(F32)
        return total

    def s2(c):
        for d in (1, 2, 3):
            x1(c, d).wait_recv()
        z_send[c] = reduce_x(c, part, part_in, (1 - zl) * half).astype(BF16)
        z1(c).start()
        row_sum[c] = reduce_x(c, part, part_in, zl * half)

    def s3(c):
        z1(c).wait_recv()
        grad = row_sum[c] + z_in[c].astype(F32) - target[rows_of(zl, half), pl.ds(pl.multiple_of(c * CW, CW), CW)]
        gsq[c, rows_of(row, half), :] = (grad * grad).astype(BF16)
        z2(c).start()

    def s4(c):
        z2(c).wait_recv()
        for d in (1, 2, 3):
            x2(c, d).start()

    def s5(c):
        for d in (1, 2, 3):
            x2(c, d).wait_recv()
        for q in range(ZH):
            rows = pl.ds(q * piece, piece)
            fisher = jnp.dot(asq_t[rows, :], gsq[c], preferred_element_type=F32)
            nd[c, 0, rows, :] = (fisher * w[c, rows, :].astype(F32)).astype(BF16)
            nd[c, 1, rows, :] = fisher.astype(BF16)
        across(c).start()

    def s6(c):
        across(c).wait_recv()

        def add(k, step):
            rows = z_piece(step)
            nd_sum[c, k, rows, :] = (nd[c, k, rows, mine].astype(F32) + nd_in[c, k, rows, :].astype(F32)).astype(BF16)

        add(0, 2)
        far(c, 0).start()
        add(1, 2)
        far(c, 1).start()
        add(1, 1)
        near(c, 0).start()
        add(0, -1)
        near(c, 1).start()
        add(0, 1)
        add(1, -1)
        add(0, 0)
        add(1, 0)

    def s7(c):
        for k in range(2):
            far(c, k).wait_recv()
            rows = z_piece(1 - 2 * k)
            nd_sum[c, k, rows, :] = (nd_sum[c, k, rows, :].astype(F32) + far_in[c, k].astype(F32)).astype(BF16)
            summed(c, k).start()

    def s8(c):
        for k in range(2):
            near(c, k).wait_recv()
            summed(c, k).wait_recv()
        rows = z_piece(0)
        numer = nd_sum[c, 0, rows, :].astype(F32) + near_in[c, 1].astype(F32) + sum_in[c, 0].astype(F32)
        denom = nd_sum[c, 1, rows, :].astype(F32) + near_in[c, 0].astype(F32) + sum_in[c, 1].astype(F32)
        merged[c, rows, mine] = (numer / (denom + 1e-6)).astype(BF16)
        spread(c, 0).start()
        spread(c, 1).start()
        share(c, 0).start()

    def s9(c):
        spread(c, 0).wait_recv()
        spread(c, 1).wait_recv()
        forward(c).start()
        share(c, 1).start()
        share(c, 3).start()

    def s10(c):
        forward(c).wait_recv()
        share(c, 2).start()

    def s11(c):
        for step in range(ZH):
            share(c, step).wait_recv()
        product(acts, c, merged, part2)
        for d in (1, 2, 3):
            x3(c, d).start()
        store(c).start()

    def s12(c):
        for d in (1, 2, 3):
            x3(c, d).wait_recv()
        z_send2[c] = reduce_x(c, part2, part2_in, (1 - zl) * half).astype(BF16)
        z3(c).start()
        row_sum2[c] = reduce_x(c, part2, part2_in, zl * half)

    def s13(c):
        z3(c).wait_recv()
        out[:, pl.ds(pl.multiple_of(c * CW, CW), CW)] = (row_sum2[c] + z_in2[c].astype(F32)).astype(BF16)

    stages = [s2, s3, s4, s5, s6, s7, s8, s9, s10, s11, s12, s13]

    @pl.loop(0, chunks + len(stages) - 1)
    def _(tick):
        for k in reversed(range(len(stages))):
            c = tick - k

            @pl.when((c >= 0) & (c < chunks))
            def _():
                stages[k](c)

    for h in range(2):
        for copy in (up, down, onward):
            copy[h].wait_send()

    @pl.loop(0, chunks)
    def _(c):
        for d in (1, 2, 3):
            x1(c, d).wait_send()
            x2(c, d).wait_send()
            x3(c, d).wait_send()
        for copy in (z1, z2, z3, across, forward):
            copy(c).wait_send()
        for k in range(2):
            for copy in (far, near, summed, spread):
                copy(c, k).wait_send()
        for step in range(ZH):
            share(c, step).wait_send()
        store(c).wait()


def local(activations, weights, labels, prototypes):
    units = activations.shape[2]
    tok, wide = labels.shape[1], weights.shape[2]
    chunks, block, half, piece = wide // CW, tok // XS, tok // XS // 2, units // ZH

    def vmem(*shape, kind=BF16):
        return pltpu.VMEM(shape, kind)

    anywhere = pl.BlockSpec(memory_space=pl.ANY)
    inside = pl.BlockSpec(memory_space=pltpu.VMEM)
    merged, result = pl.pallas_call(
        functools.partial(kernel, chunks),
        out_shape=(
            jax.ShapeDtypeStruct((units, wide), BF16),
            jax.ShapeDtypeStruct((half, wide), BF16),
        ),
        in_specs=[anywhere] * 4,
        out_specs=(anywhere, inside),
        scratch_shapes=[
            vmem(1, tok, kind=jnp.int32),
            vmem(prototypes.shape[1], wide),
            vmem(YS, units, tok // YS),
            vmem(tok, units),
            vmem(chunks, units, CW),
            vmem(units, tok),
            vmem(block, wide, kind=F32),
            vmem(chunks, tok, CW),
            vmem(chunks, XS - 1, block, CW),
            vmem(chunks, half, CW, kind=F32),
            vmem(chunks, half, CW),
            vmem(chunks, half, CW),
            vmem(chunks, tok, CW),
            vmem(chunks, 2, units, CW),
            vmem(chunks, 2, units, HALF),
            vmem(chunks, 2, units, HALF),
            vmem(chunks, 2, piece, HALF),
            vmem(chunks, 2, piece, HALF),
            vmem(chunks, 2, piece, HALF),
            vmem(chunks, units, CW),
            vmem(chunks, tok, CW),
            vmem(chunks, XS - 1, block, CW),
            vmem(chunks, half, CW, kind=F32),
            vmem(chunks, half, CW),
            vmem(chunks, half, CW),
            pltpu.SemaphoreType.DMA((chunks, SLOTS)),
            pltpu.SemaphoreType.DMA((chunks, SLOTS)),
            pltpu.SemaphoreType.DMA((3, 2)),
            pltpu.SemaphoreType.DMA((3, 2)),
            pltpu.SemaphoreType.DMA((chunks + 3,)),
            pltpu.SemaphoreType.DMA((chunks,)),
        ],
        compiler_params=pltpu.CompilerParams(
            collective_id=0, has_side_effects=True, vmem_limit_bytes=60 << 20
        ),
    )(activations[0].T, weights[0], labels, prototypes[0])
    return merged, result[None]


def solution(mesh):
    placed = (
        P("task", "col", "row"),
        P("task", "row", "col"),
        P("task", None),
        P("task", None, "col"),
    )
    return jax.shard_map(
        local,
        mesh=mesh,
        in_specs=placed,
        out_specs=(P("row", "col"), P("task", "row", "col")),
        check_vma=False,
    )
```

```python
import functools

import jax
import jax.numpy as jnp
from jax import lax
from jax.experimental import pallas as pl
from jax.experimental.pallas import tpu as pltpu
from jax.sharding import PartitionSpec as P

MESH = pl.DeviceIdType.MESH
F32, BF16 = jnp.float32, jnp.bfloat16
ZH, XS, YS = 4, 4, 4
CW = 256
HALF = CW // 2

X1, Z1, Z2, X2, CORE, PLAIN, FAR, NEAR, SUM, MERGED, FORWARD, SHARE, X3, Z3 = 0, 3, 4, 5, 8, 9, 10, 11, 12, 13, 15, 16, 20, 23
G_Z, G_ON, G_PAIR, G_X = 24, 26, 27, 28
SLOTS = 31


def kernel(
    chunks, acts_in, w_in, labels_in, protos_in, merged_out, out,
    labels, protos, acts_t, acts, w, asq_t, target, part, part_in, row_sum, z_send, z_in, gsq, quarter, asq_q, plain, plain_out, plain_in,
    nd, nd_in, nd_sum, far_in, near_in, sum_in, merged, part2, part2_in, row_sum2, z_send2, z_in2,
    send_sem, recv_sem, gather_send, gather_recv, early_send, early_recv, local_sem, store_sem,
):
    task, row, y = lax.axis_index("task"), lax.axis_index("row"), lax.axis_index("col")
    zh, core = task // 2, task % 2
    x, zl = row // 2, row % 2
    tok, units = acts.shape
    block = tok // XS
    half = block // 2
    piece = units // ZH

    def at_x(step):
        return {"row": (x + step) % XS * 2 + zl}

    pair = {"row": x * 2 + 1 - zl}
    twin = {"task": zh * 2 + 1 - core}

    def at_z(step):
        return {"task": (zh + step + ZH) % ZH * 2 + core}

    way = 1 - 2 * core

    def at_y(step):
        return {"col": (y + step + YS) % YS}

    def rows_of(index, size):
        return pl.ds(pl.multiple_of(index * size, size), size)

    def z_piece(step):
        return rows_of((zh + step + ZH) % ZH, piece)

    mine = pl.ds(pl.multiple_of(core * HALF, HALF), HALF)
    others = pl.ds(pl.multiple_of((1 - core) * HALF, HALF), HALF)

    def remote(src, dst, c, slot, device):
        return pltpu.make_async_remote_copy(
            src_ref=src, dst_ref=dst, send_sem=send_sem.at[c, slot], recv_sem=recv_sem.at[c, slot],
            device_id=device, device_id_type=MESH,
        )

    def x1(c, d):
        return remote(part.at[c, rows_of((x + d) % XS, block)], part_in.at[c, d - 1], c, X1 + d - 1, at_x(d))

    def z1(c):
        return remote(z_send.at[c], z_in.at[c], c, Z1, pair)

    def z2(c):
        here = gsq.at[c, 0, rows_of(row, half)]
        return remote(here, here, c, Z2, pair)

    def x2(c, d):
        here = gsq.at[c, 0, rows_of(x, block)]
        return remote(here, here, c, X2 + d - 1, at_x(d))

    def g_z(c, k):
        rows = rows_of(row, half)
        return remote(gsq.at[c, 0, rows], gsq.at[c, 3 - 2 * k, rows], c, G_Z + k, at_z(1 - 2 * k))

    def g_on(c):
        rows = rows_of(row, half)
        return remote(gsq.at[c, 3 - 2 * core, rows], gsq.at[c, 2, rows], c, G_ON, at_z(way))

    def g_pair(c):
        here = gsq.at[c, pl.ds(1, ZH - 1), rows_of(row, half)]
        return remote(here, here, c, G_PAIR, pair)

    def g_x(c, d):
        here = gsq.at[c, pl.ds(1, ZH - 1), rows_of(x, block)]
        return remote(here, here, c, G_X + d - 1, at_x(d))

    def across(c):
        return remote(nd.at[c, :, others], nd_in.at[c], c, CORE, twin)

    def across_plain(c):
        return remote(plain_out.at[c, :, others], plain_in.at[c], c, PLAIN, twin)

    def far(c):
        return remote(nd_sum.at[c, z_piece(2)], far_in.at[c], c, FAR, at_z(way))

    def near(c):
        return remote(nd_sum.at[c, z_piece(-way)], near_in.at[c], c, NEAR, at_z(-way))

    def summed(c):
        return remote(nd_sum.at[c, z_piece(way)], sum_in.at[c], c, SUM, at_z(way))

    def spread(c, k):
        here = merged.at[c, z_piece(0), mine]
        return remote(here, here, c, MERGED + k, at_z(1 - 2 * k))

    def forward(c):
        here = merged.at[c, z_piece(-way), mine]
        return remote(here, here, c, FORWARD, at_z(way))

    def share(c, step):
        here = merged.at[c, z_piece(step), mine]
        return remote(here, here, c, SHARE + step, twin)

    def x3(c, d):
        return remote(part2.at[c, rows_of((x + d) % XS, block)], part2_in.at[c, d - 1], c, X3 + d - 1, at_x(d))

    def z3(c):
        return remote(z_send2.at[c], z_in2.at[c], c, Z3, pair)

    def store(c):
        return pltpu.make_async_copy(
            merged.at[c], merged_out.at[:, pl.ds(pl.multiple_of(c * CW, CW), CW)], store_sem.at[c]
        )

    load_acts = pltpu.make_async_copy(acts_in, acts_t.at[y], local_sem.at[chunks])
    load_acts.start()
    loads = [
        pltpu.make_async_copy(w_in.at[:, pl.ds(c * CW, CW)], w.at[c], local_sem.at[c]) for c in range(chunks)
    ]
    for load in loads:
        load.start()
    small = [
        pltpu.make_async_copy(labels_in, labels, local_sem.at[chunks + 1]),
        pltpu.make_async_copy(protos_in, protos, local_sem.at[chunks + 2]),
    ]
    for load in small:
        load.start()

    barrier = pltpu.get_barrier_semaphore()
    peers = [at(step) for at in (at_x, at_y, at_z) for step in (1, 2, 3)] + [pair, twin]
    for peer in peers:
        pl.semaphore_signal(barrier, inc=1, device_id=peer, device_id_type=MESH)
    pl.semaphore_wait(barrier, len(peers))

    pieces = [pl.ds(0, units // 2), pl.ds(units // 2, units // 2)]

    def gather(src, index, slot, h, device):
        return pltpu.make_async_remote_copy(
            src_ref=src.at[pieces[h]], dst_ref=acts_t.at[index, pieces[h]], send_sem=gather_send.at[slot, h],
            recv_sem=gather_recv.at[slot, h], device_id=device, device_id_type=MESH,
        )

    up = [gather(acts_in, y, 0, h, at_y(1)) for h in range(2)]
    down = [gather(acts_in, y, 1, h, at_y(-1)) for h in range(2)]
    source = (y + 2 * core - 1 + YS) % YS
    onward = [gather(acts_t.at[source], source, 2, h, at_y(1 - 2 * core)) for h in range(2)]
    for h in range(2):
        up[h].start()
        down[h].start()

    def early(src, dst, slot, device):
        return pltpu.make_async_remote_copy(
            src_ref=src, dst_ref=dst, send_sem=early_send.at[slot], recv_sem=early_recv.at[slot],
            device_id=device, device_id_type=MESH,
        )

    over_z = [early(acts_in.at[z_piece(k)], quarter.at[y, ZH - 1 - k], k - 1, at_z(k)) for k in (1, 2, 3)]
    over_y = [early(quarter.at[y], quarter.at[y], 2 + d, at_y(d)) for d in (1, 2, 3)]
    for copy in over_z:
        copy.start()

    def tokens(index):
        rows = rows_of(index, block)
        turned = acts_t[index]
        acts[rows, :] = turned.T
        wide = turned.astype(F32)
        asq_t[:, rows] = (wide * wide).astype(BF16)
        step = (index - x + XS) % XS

        @pl.loop(0, chunks)
        def _(c):
            part[c, rows, :] = jnp.dot(acts[rows, :], w[c], preferred_element_type=F32).astype(BF16)

            @pl.when(step != 0)
            def _():
                x1(c, step).start()

    for load in small:
        load.wait()
    onehot = (
        labels[:, rows_of(x, block)] == lax.broadcasted_iota(jnp.int32, (protos.shape[0], block), 0)
    ).astype(F32).astype(BF16)
    target[...] = lax.dot_general(onehot, protos[...], (((0,), (0,)), ((), ())), preferred_element_type=F32)

    load_acts.wait()
    for load in loads:
        load.wait()
    tokens(y)
    for h in range(2):
        up[h].wait_recv()
        down[h].wait_recv()
        onward[h].start()
    for copy in over_z:
        copy.wait_recv()
    for copy in over_y:
        copy.start()
    tokens((y + 1) % YS)
    tokens((y + 3) % YS)
    for h in range(2):
        onward[h].wait_recv()
    tokens((y + 2) % YS)

    def product(left, c, right, result):
        for m in range(2):
            rows = pl.ds(m * (tok // 2), tok // 2)
            result[c, rows, :] = jnp.dot(left[rows, :], right[c], preferred_element_type=F32).astype(BF16)

    def reduce_x(c, own_part, arrived, start):
        rows = pl.ds(pl.multiple_of(start, half), half)
        total = own_part[c, pl.ds(pl.multiple_of(x * block + start, half), half), :].astype(F32)
        for d in range(XS - 1):
            total = total + arrived[c, d, rows, :].astype(F32)
        return total

    def s2(c):
        for d in (1, 2, 3):
            x1(c, d).wait_recv()
        z_send[c] = reduce_x(c, part, part_in, (1 - zl) * half).astype(BF16)
        z1(c).start()
        row_sum[c] = reduce_x(c, part, part_in, zl * half)

    def s3(c):
        z1(c).wait_recv()
        grad = row_sum[c] + z_in[c].astype(F32) - target[rows_of(zl, half), pl.ds(pl.multiple_of(c * CW, CW), CW)]
        gsq[c, 0, rows_of(row, half), :] = (grad * grad).astype(BF16)
        z2(c).start()
        for k in range(2):
            g_z(c, k).start()

    def s4(c):
        z2(c).wait_recv()
        for d in (1, 2, 3):
            x2(c, d).start()
        for k in range(2):
            g_z(c, k).wait_recv()
        g_on(c).start()

    def s5(c):
        for d in (1, 2, 3):
            x2(c, d).wait_recv()
        for q in range(ZH):
            rows = pl.ds(q * piece, piece)
            fisher = jnp.dot(asq_t[rows, :], gsq[c, 0], preferred_element_type=F32)
            nd[c, rows, :] = (fisher * w[c, rows, :].astype(F32)).astype(BF16)
        across(c).start()
        g_on(c).wait_recv()
        g_pair(c).start()

    def s6(c):
        across(c).wait_recv()

        def add(step):
            rows = z_piece(step)
            nd_sum[c, rows, :] = (nd[c, rows, mine].astype(F32) + nd_in[c, rows, :].astype(F32)).astype(BF16)

        add(2)
        far(c).start()
        add(-way)
        near(c).start()
        add(way)
        add(0)
        g_pair(c).wait_recv()
        for d in (1, 2, 3):
            g_x(c, d).start()

    def s7(c):
        far(c).wait_recv()
        rows = z_piece(way)
        nd_sum[c, rows, :] = (nd_sum[c, rows, :].astype(F32) + far_in[c].astype(F32)).astype(BF16)
        summed(c).start()

        @pl.when(c == 0)
        def _():
            for copy in over_y:
                copy.wait_recv()

            @pl.loop(0, YS)
            def _(b):
                for k in range(ZH - 1):
                    wide = quarter[b, k].astype(F32)
                    asq_q[k, :, rows_of(b, block)] = (wide * wide).astype(BF16)

        for d in (1, 2, 3):
            g_x(c, d).wait_recv()
        total = jnp.dot(asq_t[z_piece(0), :], gsq[c, 0], preferred_element_type=F32)
        for k in range(1, ZH):
            total = total + jnp.dot(asq_q[k - 1], gsq[c, k], preferred_element_type=F32)
        plain[c] = total
        plain_out[c] = total.astype(BF16)
        across_plain(c).start()

    def s8(c):
        for copy in (near, summed, across_plain):
            copy(c).wait_recv()
        rows = z_piece(0)
        numer = nd_sum[c, rows, :].astype(F32) + near_in[c].astype(F32) + sum_in[c].astype(F32)
        denom = plain[c, :, mine] + plain_in[c].astype(F32)
        merged[c, rows, mine] = (numer / (denom + 1e-6)).astype(BF16)
        spread(c, 0).start()
        spread(c, 1).start()
        share(c, 0).start()

    def s9(c):
        spread(c, 0).wait_recv()
        spread(c, 1).wait_recv()
        forward(c).start()
        share(c, 1).start()
        share(c, 3).start()

    def s10(c):
        forward(c).wait_recv()
        share(c, 2).start()

    def s11(c):
        for step in range(ZH):
            share(c, step).wait_recv()
        product(acts, c, merged, part2)
        for d in (1, 2, 3):
            x3(c, d).start()
        store(c).start()

    def s12(c):
        for d in (1, 2, 3):
            x3(c, d).wait_recv()
        z_send2[c] = reduce_x(c, part2, part2_in, (1 - zl) * half).astype(BF16)
        z3(c).start()
        row_sum2[c] = reduce_x(c, part2, part2_in, zl * half)

    def s13(c):
        z3(c).wait_recv()
        out[:, pl.ds(pl.multiple_of(c * CW, CW), CW)] = (row_sum2[c] + z_in2[c].astype(F32)).astype(BF16)

    stages = [s2, s3, s4, s5, s6, s7, s8, s9, s10, s11, s12, s13]

    @pl.loop(0, chunks + len(stages) - 1)
    def _(tick):
        for k in reversed(range(len(stages))):
            c = tick - k

            @pl.when((c >= 0) & (c < chunks))
            def _():
                stages[k](c)

    for h in range(2):
        for copy in (up, down, onward):
            copy[h].wait_send()
    for copy in over_z + over_y:
        copy.wait_send()

    @pl.loop(0, chunks)
    def _(c):
        for d in (1, 2, 3):
            x1(c, d).wait_send()
            x2(c, d).wait_send()
            x3(c, d).wait_send()
            g_x(c, d).wait_send()
        for copy in (z1, z2, z3, across, across_plain, far, near, summed, forward, g_on, g_pair):
            copy(c).wait_send()
        for k in range(2):
            spread(c, k).wait_send()
            g_z(c, k).wait_send()
        for step in range(ZH):
            share(c, step).wait_send()
        store(c).wait()


def local(activations, weights, labels, prototypes):
    units = activations.shape[2]
    tok, wide = labels.shape[1], weights.shape[2]
    chunks, block, half, piece = wide // CW, tok // XS, tok // XS // 2, units // ZH

    def vmem(*shape, kind=BF16):
        return pltpu.VMEM(shape, kind)

    anywhere = pl.BlockSpec(memory_space=pl.ANY)
    inside = pl.BlockSpec(memory_space=pltpu.VMEM)
    merged, result = pl.pallas_call(
        functools.partial(kernel, chunks),
        out_shape=(
            jax.ShapeDtypeStruct((units, wide), BF16),
            jax.ShapeDtypeStruct((half, wide), BF16),
        ),
        in_specs=[anywhere] * 4,
        out_specs=(anywhere, inside),
        scratch_shapes=[
            vmem(1, tok, kind=jnp.int32),
            vmem(prototypes.shape[1], wide),
            vmem(YS, units, tok // YS),
            vmem(tok, units),
            vmem(chunks, units, CW),
            vmem(units, tok),
            vmem(block, wide, kind=F32),
            vmem(chunks, tok, CW),
            vmem(chunks, XS - 1, block, CW),
            vmem(chunks, half, CW, kind=F32),
            vmem(chunks, half, CW),
            vmem(chunks, half, CW),
            vmem(chunks, ZH, tok, CW),
            vmem(YS, ZH - 1, piece, tok // YS),
            vmem(ZH - 1, piece, tok),
            vmem(chunks, piece, CW, kind=F32),
            vmem(chunks, piece, CW),
            vmem(chunks, piece, HALF),
            vmem(chunks, units, CW),
            vmem(chunks, units, HALF),
            vmem(chunks, units, HALF),
            vmem(chunks, piece, HALF),
            vmem(chunks, piece, HALF),
            vmem(chunks, piece, HALF),
            vmem(chunks, units, CW),
            vmem(chunks, tok, CW),
            vmem(chunks, XS - 1, block, CW),
            vmem(chunks, half, CW, kind=F32),
            vmem(chunks, half, CW),
            vmem(chunks, half, CW),
            pltpu.SemaphoreType.DMA((chunks, SLOTS)),
            pltpu.SemaphoreType.DMA((chunks, SLOTS)),
            pltpu.SemaphoreType.DMA((3, 2)),
            pltpu.SemaphoreType.DMA((3, 2)),
            pltpu.SemaphoreType.DMA((6,)),
            pltpu.SemaphoreType.DMA((6,)),
            pltpu.SemaphoreType.DMA((chunks + 3,)),
            pltpu.SemaphoreType.DMA((chunks,)),
        ],
        compiler_params=pltpu.CompilerParams(
            collective_id=0, has_side_effects=True, vmem_limit_bytes=60 << 20
        ),
    )(activations[0].T, weights[0], labels, prototypes[0])
    return merged, result[None]


def solution(mesh):
    placed = (
        P("task", "col", "row"),
        P("task", "row", "col"),
        P("task", None),
        P("task", None, "col"),
    )
    return jax.shard_map(
        local,
        mesh=mesh,
        in_specs=placed,
        out_specs=(P("row", "col"), P("task", "row", "col")),
        check_vma=False,
    )
```

```python
import functools

import jax
import jax.numpy as jnp
from jax import lax
from jax.experimental import pallas as pl
from jax.experimental.pallas import tpu as pltpu
from jax.sharding import PartitionSpec as P

MESH = pl.DeviceIdType.MESH
F32, BF16 = jnp.float32, jnp.bfloat16
ZH, XS, YS = 4, 4, 4
CW = 256
HALF = CW // 2

X1, Z1, X2, CORE, PLAIN, FAR, NEAR, SUM, MERGED, FORWARD, SHARE, X3, Z3 = 0, 3, 4, 7, 8, 9, 10, 11, 12, 14, 15, 19, 22
RING, RING_END, G_X = 23, 29, 30
SLOTS = 39


def kernel(
    chunks, acts_in, w_in, labels_in, protos_in, merged_out, out,
    labels, protos, acts_t, acts, w, asq_t, target, part, part_in, row_sum, z_send, z_in, gsq, quarter, asq_q, plain, plain_out, plain_in,
    w_early, weighted, weighted_out, weighted_in, nd, nd_in, nd_sum, far_in, near_in, sum_in, merged, part2, part2_in, row_sum2, z_send2, z_in2,
    send_sem, recv_sem, gather_send, gather_recv, early_send, early_recv, local_sem, store_sem,
):
    task, row, y = lax.axis_index("task"), lax.axis_index("row"), lax.axis_index("col")
    zh, core = task // 2, task % 2
    x, zl = row // 2, row % 2
    place = zh * 2 + zl
    last = chunks - 1
    tok, units = acts.shape
    block = tok // XS
    half = block // 2
    piece = units // ZH

    def at_x(step):
        return {"row": (x + step) % XS * 2 + zl}

    pair = {"row": x * 2 + 1 - zl}
    twin = {"task": zh * 2 + 1 - core}

    def at_z(step):
        return {"task": (zh + step + ZH) % ZH * 2 + core}

    way = 1 - 2 * core

    def at_y(step):
        return {"col": (y + step + YS) % YS}

    def rows_of(index, size):
        return pl.ds(pl.multiple_of(index * size, size), size)

    def z_piece(step):
        return rows_of((zh + step + ZH) % ZH, piece)

    mine = pl.ds(pl.multiple_of(core * HALF, HALF), HALF)
    others = pl.ds(pl.multiple_of((1 - core) * HALF, HALF), HALF)

    def remote(src, dst, c, slot, device):
        return pltpu.make_async_remote_copy(
            src_ref=src, dst_ref=dst, send_sem=send_sem.at[c, slot], recv_sem=recv_sem.at[c, slot],
            device_id=device, device_id_type=MESH,
        )

    def x1(c, d):
        return remote(part.at[c, rows_of((x + d) % XS, block)], part_in.at[c, d - 1], c, X1 + d - 1, at_x(d))

    def z1(c):
        return remote(z_send.at[c], z_in.at[c], c, Z1, pair)

    def ring(step):
        spot = (place + step + 2 * ZH) % (2 * ZH)
        return spot // 2, x * 2 + spot % 2

    def at_ring(step):
        z, r = ring(step)
        return {"task": z * 2 + core, "row": r}

    def pass_on(c, hop, k):
        z, r = ring((2 * k - 1) * (hop - 1))
        here = gsq.at[c, z, rows_of(r, half)]
        return remote(here, here, c, RING + 2 * (hop - 1) + k, at_ring(1 - 2 * k))

    def pass_last(c):
        z, r = ring(-3 * way)
        here = gsq.at[c, z, rows_of(r, half)]
        return remote(here, here, c, RING_END, at_ring(way))

    def x2(c, d):
        here = gsq.at[c, zh, rows_of(x, block)]
        return remote(here, here, c, X2 + d - 1, at_x(d))

    def g_x(c, k, d):
        here = gsq.at[c, (zh + k) % ZH, rows_of(x, block)]
        return remote(here, here, c, G_X + 3 * (k - 1) + d - 1, at_x(d))

    def across(c):
        return remote(nd.at[c, :, others], nd_in.at[c], c, CORE, twin)

    def across_weighted(c):
        return remote(weighted_out.at[:, others], weighted_in, c, CORE, twin)

    def across_plain(c):
        return remote(plain_out.at[c, :, others], plain_in.at[c], c, PLAIN, twin)

    def far(c):
        return remote(nd_sum.at[c, z_piece(2)], far_in.at[c], c, FAR, at_z(way))

    def near(c):
        return remote(nd_sum.at[c, z_piece(-way)], near_in.at[c], c, NEAR, at_z(-way))

    def summed(c):
        return remote(nd_sum.at[c, z_piece(way)], sum_in.at[c], c, SUM, at_z(way))

    def spread(c, k):
        here = merged.at[c, z_piece(0), mine]
        return remote(here, here, c, MERGED + k, at_z(1 - 2 * k))

    def forward(c):
        here = merged.at[c, z_piece(-way), mine]
        return remote(here, here, c, FORWARD, at_z(way))

    def share(c, step):
        here = merged.at[c, z_piece(step), mine]
        return remote(here, here, c, SHARE + step, twin)

    def x3(c, d):
        return remote(part2.at[c, rows_of((x + d) % XS, block)], part2_in.at[c, d - 1], c, X3 + d - 1, at_x(d))

    def z3(c):
        return remote(z_send2.at[c], z_in2.at[c], c, Z3, pair)

    def store(c):
        return pltpu.make_async_copy(
            merged.at[c], merged_out.at[:, pl.ds(pl.multiple_of(c * CW, CW), CW)], store_sem.at[c]
        )

    load_acts = pltpu.make_async_copy(acts_in, acts_t.at[y], local_sem.at[chunks])
    load_acts.start()
    loads = [
        pltpu.make_async_copy(w_in.at[:, pl.ds(c * CW, CW)], w.at[c], local_sem.at[c]) for c in range(chunks)
    ]
    for load in loads:
        load.start()
    small = [
        pltpu.make_async_copy(labels_in, labels, local_sem.at[chunks + 1]),
        pltpu.make_async_copy(protos_in, protos, local_sem.at[chunks + 2]),
    ]
    for load in small:
        load.start()

    barrier = pltpu.get_barrier_semaphore()
    peers = [at(step) for at in (at_x, at_y, at_z) for step in (1, 2, 3)] + [at_ring(1), at_ring(-1), twin]
    for peer in peers:
        pl.semaphore_signal(barrier, inc=1, device_id=peer, device_id_type=MESH)
    pl.semaphore_wait(barrier, len(peers))

    pieces = [pl.ds(0, units // 2), pl.ds(units // 2, units // 2)]

    def gather(src, index, slot, h, device):
        return pltpu.make_async_remote_copy(
            src_ref=src.at[pieces[h]], dst_ref=acts_t.at[index, pieces[h]], send_sem=gather_send.at[slot, h],
            recv_sem=gather_recv.at[slot, h], device_id=device, device_id_type=MESH,
        )

    up = [gather(acts_in, y, 0, h, at_y(1)) for h in range(2)]
    down = [gather(acts_in, y, 1, h, at_y(-1)) for h in range(2)]
    source = (y + 2 * core - 1 + YS) % YS
    onward = [gather(acts_t.at[source], source, 2, h, at_y(1 - 2 * core)) for h in range(2)]
    for h in range(2):
        up[h].start()
        down[h].start()

    def early(src, dst, slot, device):
        return pltpu.make_async_remote_copy(
            src_ref=src, dst_ref=dst, send_sem=early_send.at[slot], recv_sem=early_recv.at[slot],
            device_id=device, device_id_type=MESH,
        )

    over_z = [early(acts_in.at[z_piece(k)], quarter.at[y, ZH - 1 - k], k - 1, at_z(k)) for k in (1, 2, 3)]
    over_y = [early(quarter.at[y], quarter.at[y], 2 + d, at_y(d)) for d in (1, 2, 3)]
    weights_z = [
        early(w_in.at[z_piece(k), pl.ds(last * CW, CW)], w_early.at[ZH - 1 - k], 5 + k, at_z(k)) for k in (1, 2, 3)
    ]
    for copy in over_z + weights_z:
        copy.start()

    def tokens(index):
        rows = rows_of(index, block)
        turned = acts_t[index]
        acts[rows, :] = turned.T
        wide = turned.astype(F32)
        asq_t[:, rows] = (wide * wide).astype(BF16)
        step = (index - x + XS) % XS

        @pl.loop(0, chunks)
        def _(c):
            part[c, rows, :] = jnp.dot(acts[rows, :], w[c], preferred_element_type=F32).astype(BF16)

            @pl.when(step != 0)
            def _():
                x1(c, step).start()

    for load in small:
        load.wait()
    onehot = (
        labels[:, rows_of(x, block)] == lax.broadcasted_iota(jnp.int32, (protos.shape[0], block), 0)
    ).astype(F32).astype(BF16)
    target[...] = lax.dot_general(onehot, protos[...], (((0,), (0,)), ((), ())), preferred_element_type=F32)

    load_acts.wait()
    for load in loads:
        load.wait()
    tokens(y)
    for h in range(2):
        up[h].wait_recv()
        down[h].wait_recv()
        onward[h].start()
    for copy in over_z:
        copy.wait_recv()
    for copy in over_y:
        copy.start()
    tokens((y + 1) % YS)
    tokens((y + 3) % YS)
    for h in range(2):
        onward[h].wait_recv()
    tokens((y + 2) % YS)

    def product(left, c, right, result):
        for m in range(2):
            rows = pl.ds(m * (tok // 2), tok // 2)
            result[c, rows, :] = jnp.dot(left[rows, :], right[c], preferred_element_type=F32).astype(BF16)

    def reduce_x(c, own_part, arrived, start):
        rows = pl.ds(pl.multiple_of(start, half), half)
        total = own_part[c, pl.ds(pl.multiple_of(x * block + start, half), half), :].astype(F32)
        for d in range(XS - 1):
            total = total + arrived[c, d, rows, :].astype(F32)
        return total

    def s2(c):
        for d in (1, 2, 3):
            x1(c, d).wait_recv()
        z_send[c] = reduce_x(c, part, part_in, (1 - zl) * half).astype(BF16)
        z1(c).start()
        row_sum[c] = reduce_x(c, part, part_in, zl * half)

    def s3(c):
        z1(c).wait_recv()
        grad = row_sum[c] + z_in[c].astype(F32) - target[rows_of(zl, half), pl.ds(pl.multiple_of(c * CW, CW), CW)]
        gsq[c, zh, rows_of(row, half), :] = (grad * grad).astype(BF16)
        for k in range(2):
            pass_on(c, 1, k).start()

    def s4(c):
        for k in range(2):
            pass_on(c, 1, k).wait_recv()
        for d in (1, 2, 3):
            x2(c, d).start()
        for k in range(2):
            pass_on(c, 2, k).start()

    def s5(c):
        for d in (1, 2, 3):
            x2(c, d).wait_recv()

        @pl.when(c != last)
        def _():
            for q in range(ZH):
                rows = pl.ds(q * piece, piece)
                fisher = jnp.dot(asq_t[rows, :], gsq[c, zh], preferred_element_type=F32)
                nd[c, rows, :] = (fisher * w[c, rows, :].astype(F32)).astype(BF16)
            across(c).start()

        for k in range(2):
            pass_on(c, 2, k).wait_recv()
        for k in range(2):
            pass_on(c, 3, k).start()

    def s6(c):
        @pl.when(c != last)
        def _():
            across(c).wait_recv()

            def add(step):
                rows = z_piece(step)
                nd_sum[c, rows, :] = (nd[c, rows, mine].astype(F32) + nd_in[c, rows, :].astype(F32)).astype(BF16)

            add(2)
            far(c).start()
            add(-way)
            near(c).start()
            add(way)
            add(0)

        for k in range(2):
            pass_on(c, 3, k).wait_recv()
        pass_last(c).start()
        for k in (1, 3):
            for d in (1, 2, 3):
                g_x(c, k, d).start()

    def s7(c):
        @pl.when(c != last)
        def _():
            far(c).wait_recv()
            rows = z_piece(way)
            nd_sum[c, rows, :] = (nd_sum[c, rows, :].astype(F32) + far_in[c].astype(F32)).astype(BF16)
            summed(c).start()

        pass_last(c).wait_recv()
        for d in (1, 2, 3):
            g_x(c, 2, d).start()

    def s8(c):
        @pl.when(c == 0)
        def _():
            for copy in over_y:
                copy.wait_recv()

            @pl.loop(0, YS)
            def _(b):
                for k in range(ZH - 1):
                    wide = quarter[b, k].astype(F32)
                    asq_q[k, :, rows_of(b, block)] = (wide * wide).astype(BF16)

        def fisher(k):
            squares = asq_t[z_piece(0), :] if k == 0 else asq_q[k - 1]
            return jnp.dot(squares, gsq[c, (zh + k) % ZH], preferred_element_type=F32)

        for k in (1, 3, 2):
            for d in (1, 2, 3):
                g_x(c, k, d).wait_recv()

        @pl.when(c != last)
        def _():
            total = fisher(0)
            for k in range(1, ZH):
                total = total + fisher(k)
            plain[c] = total
            plain_out[c] = total.astype(BF16)
            across_plain(c).start()

        @pl.when(c == last)
        def _():
            for copy in weights_z:
                copy.wait_recv()
            plain[c] = fisher(0)
            weighted[...] = plain[c] * w[c, z_piece(0), :].astype(F32)
            for k in range(1, ZH):
                one = fisher(k)
                plain[c] += one
                weighted[...] += one * w_early[k - 1].astype(F32)
            plain_out[c] = plain[c].astype(BF16)
            weighted_out[...] = weighted[...].astype(BF16)
            across_plain(c).start()
            across_weighted(c).start()

    def s8b(c):
        across_plain(c).wait_recv()
        rows = z_piece(0)
        denom = plain[c, :, mine] + plain_in[c].astype(F32) + 1e-6

        @pl.when(c != last)
        def _():
            near(c).wait_recv()
            summed(c).wait_recv()
            numer = nd_sum[c, rows, :].astype(F32) + near_in[c].astype(F32) + sum_in[c].astype(F32)
            merged[c, rows, mine] = (numer / denom).astype(BF16)

        @pl.when(c == last)
        def _():
            across_weighted(c).wait_recv()
            merged[c, rows, mine] = ((weighted[:, mine] + weighted_in[...].astype(F32)) / denom).astype(BF16)

        spread(c, 0).start()
        spread(c, 1).start()
        share(c, 0).start()

    def s9(c):
        spread(c, 0).wait_recv()
        spread(c, 1).wait_recv()
        forward(c).start()
        share(c, 1).start()
        share(c, 3).start()

    def s10(c):
        forward(c).wait_recv()
        share(c, 2).start()

    def s11(c):
        for step in range(ZH):
            share(c, step).wait_recv()
        product(acts, c, merged, part2)
        for d in (1, 2, 3):
            x3(c, d).start()
        store(c).start()

    def s12(c):
        for d in (1, 2, 3):
            x3(c, d).wait_recv()
        z_send2[c] = reduce_x(c, part2, part2_in, (1 - zl) * half).astype(BF16)
        z3(c).start()
        row_sum2[c] = reduce_x(c, part2, part2_in, zl * half)

    def s13(c):
        z3(c).wait_recv()
        out[:, pl.ds(pl.multiple_of(c * CW, CW), CW)] = (row_sum2[c] + z_in2[c].astype(F32)).astype(BF16)

    stages = [s2, s3, s4, s5, s6, s7, s8, s8b, s9, s10, s11, s12, s13]

    @pl.loop(0, chunks + len(stages) - 1)
    def _(tick):
        for k in reversed(range(len(stages))):
            c = tick - k

            @pl.when((c >= 0) & (c < chunks))
            def _():
                stages[k](c)

    for h in range(2):
        for copy in (up, down, onward):
            copy[h].wait_send()
    for copy in over_z + over_y + weights_z:
        copy.wait_send()

    @pl.loop(0, chunks)
    def _(c):
        for d in (1, 2, 3):
            x1(c, d).wait_send()
            x2(c, d).wait_send()
            x3(c, d).wait_send()
            for k in (1, 2, 3):
                g_x(c, k, d).wait_send()
        for copy in (z1, z3, across_plain, forward, pass_last):
            copy(c).wait_send()
        for k in range(2):
            spread(c, k).wait_send()
            for hop in (1, 2, 3):
                pass_on(c, hop, k).wait_send()

        @pl.when(c != last)
        def _():
            for copy in (across, far, near, summed):
                copy(c).wait_send()

        @pl.when(c == last)
        def _():
            across_weighted(c).wait_send()

        for step in range(ZH):
            share(c, step).wait_send()
        store(c).wait()


def local(activations, weights, labels, prototypes):
    units = activations.shape[2]
    tok, wide = labels.shape[1], weights.shape[2]
    chunks, block, half, piece = wide // CW, tok // XS, tok // XS // 2, units // ZH

    def vmem(*shape, kind=BF16):
        return pltpu.VMEM(shape, kind)

    anywhere = pl.BlockSpec(memory_space=pl.ANY)
    inside = pl.BlockSpec(memory_space=pltpu.VMEM)
    merged, result = pl.pallas_call(
        functools.partial(kernel, chunks),
        out_shape=(
            jax.ShapeDtypeStruct((units, wide), BF16),
            jax.ShapeDtypeStruct((half, wide), BF16),
        ),
        in_specs=[anywhere] * 4,
        out_specs=(anywhere, inside),
        scratch_shapes=[
            vmem(1, tok, kind=jnp.int32),
            vmem(prototypes.shape[1], wide),
            vmem(YS, units, tok // YS),
            vmem(tok, units),
            vmem(chunks, units, CW),
            vmem(units, tok),
            vmem(block, wide, kind=F32),
            vmem(chunks, tok, CW),
            vmem(chunks, XS - 1, block, CW),
            vmem(chunks, half, CW, kind=F32),
            vmem(chunks, half, CW),
            vmem(chunks, half, CW),
            vmem(chunks, ZH, tok, CW),
            vmem(YS, ZH - 1, piece, tok // YS),
            vmem(ZH - 1, piece, tok),
            vmem(chunks, piece, CW, kind=F32),
            vmem(chunks, piece, CW),
            vmem(chunks, piece, HALF),
            vmem(ZH - 1, piece, CW),
            vmem(piece, CW, kind=F32),
            vmem(piece, CW),
            vmem(piece, HALF),
            vmem(chunks, units, CW),
            vmem(chunks, units, HALF),
            vmem(chunks, units, HALF),
            vmem(chunks, piece, HALF),
            vmem(chunks, piece, HALF),
            vmem(chunks, piece, HALF),
            vmem(chunks, units, CW),
            vmem(chunks, tok, CW),
            vmem(chunks, XS - 1, block, CW),
            vmem(chunks, half, CW, kind=F32),
            vmem(chunks, half, CW),
            vmem(chunks, half, CW),
            pltpu.SemaphoreType.DMA((chunks, SLOTS)),
            pltpu.SemaphoreType.DMA((chunks, SLOTS)),
            pltpu.SemaphoreType.DMA((3, 2)),
            pltpu.SemaphoreType.DMA((3, 2)),
            pltpu.SemaphoreType.DMA((9,)),
            pltpu.SemaphoreType.DMA((9,)),
            pltpu.SemaphoreType.DMA((chunks + 3,)),
            pltpu.SemaphoreType.DMA((chunks,)),
        ],
        compiler_params=pltpu.CompilerParams(
            collective_id=0, has_side_effects=True, vmem_limit_bytes=60 << 20
        ),
    )(activations[0].T, weights[0], labels, prototypes[0])
    return merged, result[None]


def solution(mesh):
    placed = (
        P("task", "col", "row"),
        P("task", "row", "col"),
        P("task", None),
        P("task", None, "col"),
    )
    return jax.shard_map(
        local,
        mesh=mesh,
        in_specs=placed,
        out_specs=(P("row", "col"), P("task", "row", "col")),
        check_vma=False,
    )
```

```python
import functools

import jax
import jax.numpy as jnp
from jax import lax
from jax.experimental import pallas as pl
from jax.experimental.pallas import tpu as pltpu
from jax.sharding import PartitionSpec as P

MESH = pl.DeviceIdType.MESH
F32, BF16 = jnp.float32, jnp.bfloat16
ZH, XS, YS = 4, 4, 4
CW = 256
HALF = CW // 2

X1, Z1, X2, CORE, PLAIN, FAR, NEAR, SUM, MERGED, FORWARD, SHARE, X3, Z3 = 0, 3, 4, 7, 8, 9, 10, 11, 12, 14, 15, 19, 22
RING, RING_END, G_X = 23, 29, 30
SLOTS = 39


def kernel(
    chunks, acts_in, w_in, labels_in, protos_in, merged_out, out,
    labels, protos, acts_t, acts, w, asq_t, target, part, part_in, row_sum, z_send, z_in, gsq, quarter, asq_q, plain, plain_out, plain_in,
    w_early, weighted, weighted_out, weighted_in, nd, nd_in, nd_sum, far_in, near_in, sum_in, merged, part2, part2_in, row_sum2, z_send2, z_in2,
    send_sem, recv_sem, gather_send, gather_recv, early_send, early_recv, local_sem, store_sem,
):
    task, row, y = lax.axis_index("task"), lax.axis_index("row"), lax.axis_index("col")
    zh, core = task // 2, task % 2
    x, zl = row // 2, row % 2
    place = zh * 2 + zl
    last = chunks - 1
    tok, units = acts.shape
    block = tok // XS
    half = block // 2
    piece = units // ZH

    def at_x(step):
        return {"row": (x + step) % XS * 2 + zl}

    pair = {"row": x * 2 + 1 - zl}
    twin = {"task": zh * 2 + 1 - core}

    def at_z(step):
        return {"task": (zh + step + ZH) % ZH * 2 + core}

    way = 1 - 2 * core

    def at_y(step):
        return {"col": (y + step + YS) % YS}

    def rows_of(index, size):
        return pl.ds(pl.multiple_of(index * size, size), size)

    def z_piece(step):
        return rows_of((zh + step + ZH) % ZH, piece)

    mine = pl.ds(pl.multiple_of(core * HALF, HALF), HALF)
    others = pl.ds(pl.multiple_of((1 - core) * HALF, HALF), HALF)

    def remote(src, dst, c, slot, device):
        return pltpu.make_async_remote_copy(
            src_ref=src, dst_ref=dst, send_sem=send_sem.at[c, slot], recv_sem=recv_sem.at[c, slot],
            device_id=device, device_id_type=MESH,
        )

    def x1(c, d):
        return remote(part.at[c, rows_of((x + d) % XS, block)], part_in.at[c, d - 1], c, X1 + d - 1, at_x(d))

    def z1(c):
        return remote(z_send.at[c], z_in.at[c], c, Z1, pair)

    def ring(step):
        spot = (place + step + 2 * ZH) % (2 * ZH)
        return spot // 2, x * 2 + spot % 2

    def at_ring(step):
        z, r = ring(step)
        return {"task": z * 2 + core, "row": r}

    def pass_on(c, hop, k):
        z, r = ring((2 * k - 1) * (hop - 1))
        here = gsq.at[c, z, rows_of(r, half)]
        return remote(here, here, c, RING + 2 * (hop - 1) + k, at_ring(1 - 2 * k))

    def pass_last(c):
        z, r = ring(3 - 6 * zl)
        here = gsq.at[c, z, rows_of(r, half)]
        return remote(here, here, c, RING_END, at_ring(2 * zl - 1))

    def x2(c, d):
        here = gsq.at[c, zh, rows_of(x, block)]
        return remote(here, here, c, X2 + d - 1, at_x(d))

    def g_x(c, k, d):
        here = gsq.at[c, (zh + k) % ZH, rows_of(x, block)]
        return remote(here, here, c, G_X + 3 * (k - 1) + d - 1, at_x(d))

    def across(c):
        return remote(nd.at[c, :, others], nd_in.at[c], c, CORE, twin)

    def across_weighted(c):
        return remote(weighted_out.at[:, others], weighted_in, c, CORE, twin)

    def across_plain(c):
        return remote(plain_out.at[c, :, others], plain_in.at[c], c, PLAIN, twin)

    def far(c):
        return remote(nd_sum.at[c, z_piece(2)], far_in.at[c], c, FAR, at_z(way))

    def near(c):
        return remote(nd_sum.at[c, z_piece(-way)], near_in.at[c], c, NEAR, at_z(-way))

    def summed(c):
        return remote(nd_sum.at[c, z_piece(way)], sum_in.at[c], c, SUM, at_z(way))

    def spread(c, k):
        here = merged.at[c, z_piece(0), mine]
        return remote(here, here, c, MERGED + k, at_z(1 - 2 * k))

    def forward(c):
        here = merged.at[c, z_piece(-way), mine]
        return remote(here, here, c, FORWARD, at_z(way))

    def share(c, step):
        here = merged.at[c, z_piece(step), mine]
        return remote(here, here, c, SHARE + step, twin)

    def x3(c, d):
        return remote(part2.at[c, rows_of((x + d) % XS, block)], part2_in.at[c, d - 1], c, X3 + d - 1, at_x(d))

    def z3(c):
        return remote(z_send2.at[c], z_in2.at[c], c, Z3, pair)

    def store(c):
        return pltpu.make_async_copy(
            merged.at[c], merged_out.at[:, pl.ds(pl.multiple_of(c * CW, CW), CW)], store_sem.at[c]
        )

    load_acts = pltpu.make_async_copy(acts_in, acts_t.at[y], local_sem.at[chunks])
    load_acts.start()
    loads = [
        pltpu.make_async_copy(w_in.at[:, pl.ds(c * CW, CW)], w.at[c], local_sem.at[c]) for c in range(chunks)
    ]
    for load in loads:
        load.start()
    small = [
        pltpu.make_async_copy(labels_in, labels, local_sem.at[chunks + 1]),
        pltpu.make_async_copy(protos_in, protos, local_sem.at[chunks + 2]),
    ]
    for load in small:
        load.start()

    barrier = pltpu.get_barrier_semaphore()
    peers = [at(step) for at in (at_x, at_y, at_z) for step in (1, 2, 3)] + [at_ring(1), at_ring(-1), twin]
    for peer in peers:
        pl.semaphore_signal(barrier, inc=1, device_id=peer, device_id_type=MESH)
    pl.semaphore_wait(barrier, len(peers))

    cut = (units // 2 + 127) // 128 * 128
    pieces = [pl.ds(0, cut), pl.ds(cut, units - cut)]

    def gather(src, index, slot, h, device):
        return pltpu.make_async_remote_copy(
            src_ref=src.at[pieces[h]], dst_ref=acts_t.at[index, pieces[h]], send_sem=gather_send.at[slot, h],
            recv_sem=gather_recv.at[slot, h], device_id=device, device_id_type=MESH,
        )

    up = [gather(acts_in, y, 0, h, at_y(1)) for h in range(2)]
    down = [gather(acts_in, y, 1, h, at_y(-1)) for h in range(2)]
    source = (y + 2 * core - 1 + YS) % YS
    onward = [gather(acts_t.at[source], source, 2, h, at_y(1 - 2 * core)) for h in range(2)]
    for h in range(2):
        up[h].start()
        down[h].start()

    def early(src, dst, slot, device):
        return pltpu.make_async_remote_copy(
            src_ref=src, dst_ref=dst, send_sem=early_send.at[slot], recv_sem=early_recv.at[slot],
            device_id=device, device_id_type=MESH,
        )

    over_z = [early(acts_in.at[z_piece(k)], quarter.at[y, ZH - 1 - k], k - 1, at_z(k)) for k in (1, 2, 3)]
    over_y = [early(quarter.at[y], quarter.at[y], 2 + d, at_y(d)) for d in (1, 2, 3)]
    weights_z = [
        early(w_in.at[z_piece(k), pl.ds(last * CW, CW)], w_early.at[ZH - 1 - k], 5 + k, at_z(k)) for k in (1, 2, 3)
    ]
    for copy in over_z + weights_z:
        copy.start()

    def turn(index, h):
        rows = rows_of(index, block)
        turned = acts_t[index, pieces[h]]
        acts[rows, pieces[h]] = turned.T
        wide = turned.astype(F32)
        asq_t[pieces[h], rows] = (wide * wide).astype(BF16)

    def multiply(index, c):
        rows = rows_of(index, block)
        step = (index - x + XS) % XS
        part[c, rows, :] = jnp.dot(acts[rows, :], w[c], preferred_element_type=F32).astype(BF16)

        @pl.when(step != 0)
        def _():
            x1(c, step).start()

    for load in small:
        load.wait()
    onehot = (
        labels[:, rows_of(x, block)] == lax.broadcasted_iota(jnp.int32, (protos.shape[0], block), 0)
    ).astype(F32).astype(BF16)
    target[...] = lax.dot_general(onehot, protos[...], (((0,), (0,)), ((), ())), preferred_element_type=F32)

    load_acts.wait()
    for load in loads:
        load.wait()
    turn(y, 0)
    turn(y, 1)

    @pl.loop(0, chunks)
    def _(c):
        multiply(y, c)

    beside = [(y + 1) % YS, (y + 3) % YS]
    across_y = (y + 2) % YS
    for h in range(2):
        up[h].wait_recv()
        down[h].wait_recv()
        onward[h].start()
        for index in beside:
            turn(index, h)
    for copy in over_z:
        copy.wait_recv()
    for index in beside:
        multiply(index, 0)
    for h in range(2):
        onward[h].wait_recv()
        turn(across_y, h)
    for copy in over_y:
        copy.start()
    multiply(across_y, 0)

    def product(left, c, right, result):
        for m in range(2):
            rows = pl.ds(m * (tok // 2), tok // 2)
            result[c, rows, :] = jnp.dot(left[rows, :], right[c], preferred_element_type=F32).astype(BF16)

    def reduce_x(c, own_part, arrived, start):
        rows = pl.ds(pl.multiple_of(start, half), half)
        total = own_part[c, pl.ds(pl.multiple_of(x * block + start, half), half), :].astype(F32)
        for d in range(XS - 1):
            total = total + arrived[c, d, rows, :].astype(F32)
        return total

    def s1(c):
        @pl.when(c > 0)
        def _():
            for index in beside + [across_y]:
                multiply(index, c)

    def s2(c):
        for d in (1, 2, 3):
            x1(c, d).wait_recv()
        z_send[c] = reduce_x(c, part, part_in, (1 - zl) * half).astype(BF16)
        z1(c).start()
        row_sum[c] = reduce_x(c, part, part_in, zl * half)

    def s3(c):
        z1(c).wait_recv()
        grad = row_sum[c] + z_in[c].astype(F32) - target[rows_of(zl, half), pl.ds(pl.multiple_of(c * CW, CW), CW)]
        gsq[c, zh, rows_of(row, half), :] = (grad * grad).astype(BF16)
        for k in range(2):
            pass_on(c, 1, k).start()

    def s4(c):
        for k in range(2):
            pass_on(c, 1, k).wait_recv()
        for d in (1, 2, 3):
            x2(c, d).start()
        for k in range(2):
            pass_on(c, 2, k).start()

    def s5(c):
        for d in (1, 2, 3):
            x2(c, d).wait_recv()

        @pl.when(c != last)
        def _():
            for q in range(ZH):
                rows = pl.ds(q * piece, piece)
                fisher = jnp.dot(asq_t[rows, :], gsq[c, zh], preferred_element_type=F32)
                nd[c, rows, :] = (fisher * w[c, rows, :].astype(F32)).astype(BF16)
            across(c).start()

        for k in range(2):
            pass_on(c, 2, k).wait_recv()
        for k in range(2):
            pass_on(c, 3, k).start()

    def s6(c):
        @pl.when(c != last)
        def _():
            across(c).wait_recv()

            def add(step):
                rows = z_piece(step)
                nd_sum[c, rows, :] = (nd[c, rows, mine].astype(F32) + nd_in[c, rows, :].astype(F32)).astype(BF16)

            add(2)
            far(c).start()
            add(-way)
            near(c).start()
            add(way)
            add(0)

        for k in range(2):
            pass_on(c, 3, k).wait_recv()
        pass_last(c).start()
        for k in (1, 3):
            for d in (1, 2, 3):
                g_x(c, k, d).start()

    def s7(c):
        @pl.when(c != last)
        def _():
            far(c).wait_recv()
            rows = z_piece(way)
            nd_sum[c, rows, :] = (nd_sum[c, rows, :].astype(F32) + far_in[c].astype(F32)).astype(BF16)
            summed(c).start()

        pass_last(c).wait_recv()
        for d in (1, 2, 3):
            g_x(c, 2, d).start()

    def s8(c):
        @pl.when(c == 0)
        def _():
            for copy in over_y:
                copy.wait_recv()

            @pl.loop(0, YS)
            def _(b):
                for k in range(ZH - 1):
                    wide = quarter[b, k].astype(F32)
                    asq_q[k, :, rows_of(b, block)] = (wide * wide).astype(BF16)

        def fisher(k):
            squares = asq_t[z_piece(0), :] if k == 0 else asq_q[k - 1]
            return jnp.dot(squares, gsq[c, (zh + k) % ZH], preferred_element_type=F32)

        for k in (1, 3, 2):
            for d in (1, 2, 3):
                g_x(c, k, d).wait_recv()

        @pl.when(c != last)
        def _():
            total = fisher(0)
            for k in range(1, ZH):
                total = total + fisher(k)
            plain[c] = total
            plain_out[c] = total.astype(BF16)
            across_plain(c).start()

        @pl.when(c == last)
        def _():
            for copy in weights_z:
                copy.wait_recv()
            plain[c] = fisher(0)
            weighted[...] = plain[c] * w[c, z_piece(0), :].astype(F32)
            for k in range(1, ZH):
                one = fisher(k)
                plain[c] += one
                weighted[...] += one * w_early[k - 1].astype(F32)
            plain_out[c] = plain[c].astype(BF16)
            weighted_out[...] = weighted[...].astype(BF16)
            across_plain(c).start()
            across_weighted(c).start()

    def merge(c):
        across_plain(c).wait_recv()
        rows = z_piece(0)
        denom = plain[c, :, mine] + plain_in[c].astype(F32) + 1e-6

        @pl.when(c != last)
        def _():
            near(c).wait_recv()
            summed(c).wait_recv()
            numer = nd_sum[c, rows, :].astype(F32) + near_in[c].astype(F32) + sum_in[c].astype(F32)
            merged[c, rows, mine] = (numer / denom).astype(BF16)

        @pl.when(c == last)
        def _():
            across_weighted(c).wait_recv()
            merged[c, rows, mine] = ((weighted[:, mine] + weighted_in[...].astype(F32)) / denom).astype(BF16)

        spread(c, 0).start()
        spread(c, 1).start()
        share(c, 0).start()

    def s9(c):
        spread(c, 0).wait_recv()
        spread(c, 1).wait_recv()
        forward(c).start()
        share(c, 1).start()
        share(c, 3).start()

    def s10(c):
        forward(c).wait_recv()
        share(c, 2).start()

    def s11(c):
        for step in range(ZH):
            share(c, step).wait_recv()
        store(c).start()
        product(acts, c, merged, part2)
        for d in (1, 2, 3):
            x3(c, d).start()
        sent(c)

        @pl.when(c == 0)
        def _():
            for h in range(2):
                for copy in (up, down, onward):
                    copy[h].wait_send()
            for copy in over_z + over_y + weights_z:
                copy.wait_send()

    def sent(c):
        for d in (1, 2, 3):
            x1(c, d).wait_send()
            x2(c, d).wait_send()
            for k in (1, 2, 3):
                g_x(c, k, d).wait_send()
        for copy in (z1, across_plain, forward, pass_last):
            copy(c).wait_send()
        for k in range(2):
            spread(c, k).wait_send()
            for hop in (1, 2, 3):
                pass_on(c, hop, k).wait_send()

        @pl.when(c != last)
        def _():
            for copy in (across, far, near, summed):
                copy(c).wait_send()

        @pl.when(c == last)
        def _():
            across_weighted(c).wait_send()

        for step in range(ZH):
            share(c, step).wait_send()

    def s12(c):
        for d in (1, 2, 3):
            x3(c, d).wait_recv()
        z_send2[c] = reduce_x(c, part2, part2_in, (1 - zl) * half).astype(BF16)
        z3(c).start()
        row_sum2[c] = reduce_x(c, part2, part2_in, zl * half)

    def s13(c):
        z3(c).wait_recv()
        out[:, pl.ds(pl.multiple_of(c * CW, CW), CW)] = (row_sum2[c] + z_in2[c].astype(F32)).astype(BF16)
        for d in (1, 2, 3):
            x3(c, d).wait_send()
        z3(c).wait_send()
        store(c).wait()

    stages = [s1, s2, s3, s4, s5, s6, s7, s8, merge, s9, s10, s11, s12, s13]

    @pl.loop(0, chunks + len(stages) - 1)
    def _(tick):
        for k in reversed(range(len(stages))):
            c = tick - k

            @pl.when((c >= 0) & (c < chunks))
            def _():
                stages[k](c)


def local(activations, weights, labels, prototypes):
    units = activations.shape[2]
    tok, wide = labels.shape[1], weights.shape[2]
    chunks, block, half, piece = wide // CW, tok // XS, tok // XS // 2, units // ZH

    def vmem(*shape, kind=BF16):
        return pltpu.VMEM(shape, kind)

    anywhere = pl.BlockSpec(memory_space=pl.ANY)
    inside = pl.BlockSpec(memory_space=pltpu.VMEM)
    merged, result = pl.pallas_call(
        functools.partial(kernel, chunks),
        out_shape=(
            jax.ShapeDtypeStruct((units, wide), BF16),
            jax.ShapeDtypeStruct((half, wide), BF16),
        ),
        in_specs=[anywhere] * 4,
        out_specs=(anywhere, inside),
        scratch_shapes=[
            vmem(1, tok, kind=jnp.int32),
            vmem(prototypes.shape[1], wide),
            vmem(YS, units, tok // YS),
            vmem(tok, units),
            vmem(chunks, units, CW),
            vmem(units, tok),
            vmem(block, wide, kind=F32),
            vmem(chunks, tok, CW),
            vmem(chunks, XS - 1, block, CW),
            vmem(chunks, half, CW, kind=F32),
            vmem(chunks, half, CW),
            vmem(chunks, half, CW),
            vmem(chunks, ZH, tok, CW),
            vmem(YS, ZH - 1, piece, tok // YS),
            vmem(ZH - 1, piece, tok),
            vmem(chunks, piece, CW, kind=F32),
            vmem(chunks, piece, CW),
            vmem(chunks, piece, HALF),
            vmem(ZH - 1, piece, CW),
            vmem(piece, CW, kind=F32),
            vmem(piece, CW),
            vmem(piece, HALF),
            vmem(chunks, units, CW),
            vmem(chunks, units, HALF),
            vmem(chunks, units, HALF),
            vmem(chunks, piece, HALF),
            vmem(chunks, piece, HALF),
            vmem(chunks, piece, HALF),
            vmem(chunks, units, CW),
            vmem(chunks, tok, CW),
            vmem(chunks, XS - 1, block, CW),
            vmem(chunks, half, CW, kind=F32),
            vmem(chunks, half, CW),
            vmem(chunks, half, CW),
            pltpu.SemaphoreType.DMA((chunks, SLOTS)),
            pltpu.SemaphoreType.DMA((chunks, SLOTS)),
            pltpu.SemaphoreType.DMA((3, 2)),
            pltpu.SemaphoreType.DMA((3, 2)),
            pltpu.SemaphoreType.DMA((9,)),
            pltpu.SemaphoreType.DMA((9,)),
            pltpu.SemaphoreType.DMA((chunks + 3,)),
            pltpu.SemaphoreType.DMA((chunks,)),
        ],
        compiler_params=pltpu.CompilerParams(
            collective_id=0, has_side_effects=True, vmem_limit_bytes=60 << 20
        ),
    )(activations[0].T, weights[0], labels, prototypes[0])
    return merged, result[None]


def solution(mesh):
    placed = (
        P("task", "col", "row"),
        P("task", "row", "col"),
        P("task", None),
        P("task", None, "col"),
    )
    return jax.shard_map(
        local,
        mesh=mesh,
        in_specs=placed,
        out_specs=(P("row", "col"), P("task", "row", "col")),
        check_vma=False,
    )
```

```python
import functools

import jax
import jax.numpy as jnp
from jax import lax
from jax.experimental import pallas as pl
from jax.experimental.pallas import tpu as pltpu
from jax.sharding import PartitionSpec as P

MESH = pl.DeviceIdType.MESH
F32, BF16 = jnp.float32, jnp.bfloat16
ZH, XS, YS = 4, 4, 4
CW = 256
HALF = CW // 2

X1, Z1, X2, CORE, PLAIN, FAR, NEAR, SUM, MERGED, FORWARD, SHARE, X3, Z3 = 0, 3, 4, 7, 8, 9, 10, 11, 12, 14, 15, 19, 22
RING, RING_END, G_X = 23, 29, 30
SLOTS = 39


def kernel(
    chunks, acts_in, w_in, labels_in, protos_in, merged_out, out,
    labels, protos, acts_t, acts, w, asq_t, target, part, part_in, row_sum, z_send, z_in, gsq, quarter, asq_q, plain, plain_out, plain_in,
    w_early, weighted, weighted_out, weighted_in, nd, nd_in, nd_sum, far_in, near_in, sum_in, merged, part2, part2_in, row_sum2, z_send2, z_in2,
    send_sem, recv_sem, gather_send, gather_recv, early_send, early_recv, local_sem, store_sem,
):
    task, row, y = lax.axis_index("task"), lax.axis_index("row"), lax.axis_index("col")
    zh, core = task // 2, task % 2
    x, zl = row // 2, row % 2
    place = zh * 2 + zl
    last = chunks - 1
    tok, units = acts.shape
    block = tok // XS
    half = block // 2
    piece = units // ZH

    def at_x(step):
        return {"row": (x + step) % XS * 2 + zl}

    pair = {"row": x * 2 + 1 - zl}
    twin = {"task": zh * 2 + 1 - core}

    def at_z(step):
        return {"task": (zh + step + ZH) % ZH * 2 + core}

    way = 1 - 2 * core

    def at_y(step):
        return {"col": (y + step + YS) % YS}

    def rows_of(index, size):
        return pl.ds(pl.multiple_of(index * size, size), size)

    def z_piece(step):
        return rows_of((zh + step + ZH) % ZH, piece)

    mine = pl.ds(pl.multiple_of(core * HALF, HALF), HALF)
    others = pl.ds(pl.multiple_of((1 - core) * HALF, HALF), HALF)

    def remote(src, dst, c, slot, device):
        return pltpu.make_async_remote_copy(
            src_ref=src, dst_ref=dst, send_sem=send_sem.at[c, slot], recv_sem=recv_sem.at[c, slot],
            device_id=device, device_id_type=MESH,
        )

    def x1(c, d):
        return remote(part.at[c, rows_of((x + d) % XS, block)], part_in.at[c, d - 1], c, X1 + d - 1, at_x(d))

    def z1(c):
        return remote(z_send.at[c], z_in.at[c], c, Z1, pair)

    def ring(step):
        spot = (place + step + 2 * ZH) % (2 * ZH)
        return spot // 2, x * 2 + spot % 2

    def at_ring(step):
        z, r = ring(step)
        return {"task": z * 2 + core, "row": r}

    def pass_on(c, hop, k):
        z, r = ring((2 * k - 1) * (hop - 1))
        here = gsq.at[c, z, rows_of(r, half)]
        return remote(here, here, c, RING + 2 * (hop - 1) + k, at_ring(1 - 2 * k))

    def pass_last(c):
        z, r = ring(3 - 6 * zl)
        here = gsq.at[c, z, rows_of(r, half)]
        return remote(here, here, c, RING_END, at_ring(2 * zl - 1))

    def x2(c, d):
        here = gsq.at[c, zh, rows_of(x, block)]
        return remote(here, here, c, X2 + d - 1, at_x(d))

    def g_x(c, k, d):
        here = gsq.at[c, (zh + k) % ZH, rows_of(x, block)]
        return remote(here, here, c, G_X + 3 * (k - 1) + d - 1, at_x(d))

    def across(c):
        return remote(nd.at[c, :, others], nd_in.at[c], c, CORE, twin)

    def across_weighted(c):
        return remote(weighted_out.at[:, others], weighted_in, c, CORE, twin)

    def across_plain(c):
        return remote(plain_out.at[c, :, others], plain_in.at[c], c, PLAIN, twin)

    def far(c):
        return remote(nd_sum.at[c, z_piece(2)], far_in.at[c], c, FAR, at_z(way))

    def near(c):
        return remote(nd_sum.at[c, z_piece(-way)], near_in.at[c], c, NEAR, at_z(-way))

    def summed(c):
        return remote(nd_sum.at[c, z_piece(way)], sum_in.at[c], c, SUM, at_z(way))

    def spread(c, k):
        here = merged.at[c, z_piece(0), mine]
        return remote(here, here, c, MERGED + k, at_z(1 - 2 * k))

    def forward(c):
        here = merged.at[c, z_piece(-way), mine]
        return remote(here, here, c, FORWARD, at_z(way))

    def share(c, step):
        here = merged.at[c, z_piece(step), mine]
        return remote(here, here, c, SHARE + step, twin)

    def x3(c, d):
        return remote(part2.at[c, rows_of((x + d) % XS, block)], part2_in.at[c, d - 1], c, X3 + d - 1, at_x(d))

    def z3(c):
        return remote(z_send2.at[c], z_in2.at[c], c, Z3, pair)

    def store(c):
        return pltpu.make_async_copy(
            merged.at[c], merged_out.at[:, pl.ds(pl.multiple_of(c * CW, CW), CW)], store_sem.at[c]
        )

    load_acts = pltpu.make_async_copy(acts_in, acts_t.at[y], local_sem.at[chunks])
    load_acts.start()
    loads = [
        pltpu.make_async_copy(w_in.at[:, pl.ds(c * CW, CW)], w.at[c], local_sem.at[c]) for c in range(chunks)
    ]
    for load in loads:
        load.start()
    small = [
        pltpu.make_async_copy(labels_in, labels, local_sem.at[chunks + 1]),
        pltpu.make_async_copy(protos_in, protos, local_sem.at[chunks + 2]),
    ]
    for load in small:
        load.start()

    barrier = pltpu.get_barrier_semaphore()
    peers = [at(step) for at in (at_x, at_y, at_z) for step in (1, 2, 3)] + [at_ring(1), at_ring(-1), twin]
    for peer in peers:
        pl.semaphore_signal(barrier, inc=1, device_id=peer, device_id_type=MESH)
    pl.semaphore_wait(barrier, len(peers))

    cut = (units // 2 + 127) // 128 * 128
    pieces = [pl.ds(0, cut), pl.ds(cut, units - cut)]

    def gather(src, index, slot, h, device):
        return pltpu.make_async_remote_copy(
            src_ref=src.at[pieces[h]], dst_ref=acts_t.at[index, pieces[h]], send_sem=gather_send.at[slot, h],
            recv_sem=gather_recv.at[slot, h], device_id=device, device_id_type=MESH,
        )

    up = [gather(acts_in, y, 0, h, at_y(1)) for h in range(2)]
    down = [gather(acts_in, y, 1, h, at_y(-1)) for h in range(2)]
    source = (y + 2 * core - 1 + YS) % YS
    onward = [gather(acts_t.at[source], source, 2, h, at_y(1 - 2 * core)) for h in range(2)]
    for h in range(2):
        up[h].start()
        down[h].start()

    def early(src, dst, slot, device):
        return pltpu.make_async_remote_copy(
            src_ref=src, dst_ref=dst, send_sem=early_send.at[slot], recv_sem=early_recv.at[slot],
            device_id=device, device_id_type=MESH,
        )

    over_z = [early(acts_in.at[z_piece(k)], quarter.at[y, ZH - 1 - k], k - 1, at_z(k)) for k in (1, 2, 3)]
    over_y = [early(quarter.at[y], quarter.at[y], 2 + d, at_y(d)) for d in (1, 2, 3)]
    weights_z = [
        early(w_in.at[z_piece(k), pl.ds(last * CW, CW)], w_early.at[ZH - 1 - k], 5 + k, at_z(k)) for k in (1, 2, 3)
    ]
    for copy in over_z + weights_z:
        copy.start()

    def turn(index, h):
        rows = rows_of(index, block)
        turned = acts_t[index, pieces[h]]
        acts[rows, pieces[h]] = turned.T
        wide = turned.astype(F32)
        asq_t[pieces[h], rows] = (wide * wide).astype(BF16)

    def multiply(index, c):
        rows = rows_of(index, block)
        step = (index - x + XS) % XS
        part[c, rows, :] = jnp.dot(acts[rows, :], w[c], preferred_element_type=F32).astype(BF16)

        @pl.when(step != 0)
        def _():
            x1(c, step).start()

    for load in small:
        load.wait()
    onehot = (
        labels[:, rows_of(x, block)] == lax.broadcasted_iota(jnp.int32, (protos.shape[0], block), 0)
    ).astype(F32).astype(BF16)
    target[...] = lax.dot_general(onehot, protos[...], (((0,), (0,)), ((), ())), preferred_element_type=F32)

    load_acts.wait()
    for load in loads:
        load.wait()
    turn(y, 0)
    turn(y, 1)

    @pl.loop(0, chunks)
    def _(c):
        multiply(y, c)

    beside = [(y + 1) % YS, (y + 3) % YS]
    across_y = (y + 2) % YS
    for h in range(2):
        up[h].wait_recv()
        down[h].wait_recv()
        onward[h].start()
        for index in beside:
            turn(index, h)
    for copy in over_z:
        copy.wait_recv()
    for index in beside:
        multiply(index, 0)
    for h in range(2):
        onward[h].wait_recv()
        turn(across_y, h)
    for copy in over_y:
        copy.start()
    multiply(across_y, 0)

    def product(left, c, right, result):
        for m in range(2):
            rows = pl.ds(m * (tok // 2), tok // 2)
            result[c, rows, :] = jnp.dot(left[rows, :], right[c], preferred_element_type=F32).astype(BF16)

    def reduce_x(c, own_part, arrived, start):
        rows = pl.ds(pl.multiple_of(start, half), half)
        total = own_part[c, pl.ds(pl.multiple_of(x * block + start, half), half), :].astype(F32)
        for d in range(XS - 1):
            total = total + arrived[c, d, rows, :].astype(F32)
        return total

    def s1(c):
        @pl.when(c > 0)
        def _():
            for index in beside + [across_y]:
                multiply(index, c)

    def s2(c):
        for d in (1, 2, 3):
            x1(c, d).wait_recv()
        z_send[c] = reduce_x(c, part, part_in, (1 - zl) * half).astype(BF16)
        z1(c).start()
        row_sum[c] = reduce_x(c, part, part_in, zl * half)

    def s3(c):
        z1(c).wait_recv()
        grad = row_sum[c] + z_in[c].astype(F32) - target[rows_of(zl, half), pl.ds(pl.multiple_of(c * CW, CW), CW)]
        gsq[c, zh, rows_of(row, half), :] = (grad * grad).astype(BF16)
        for k in range(2):
            pass_on(c, 1, k).start()

    def s4(c):
        for k in range(2):
            pass_on(c, 1, k).wait_recv()
        for d in (1, 2, 3):
            x2(c, d).start()
        for k in range(2):
            pass_on(c, 2, k).start()

    def s5(c):
        for d in (1, 2, 3):
            x2(c, d).wait_recv()

        @pl.when(c != last)
        def _():
            for q in range(ZH):
                rows = pl.ds(q * piece, piece)
                fisher = jnp.dot(asq_t[rows, :], gsq[c, zh], preferred_element_type=F32)
                nd[c, rows, :] = (fisher * w[c, rows, :].astype(F32)).astype(BF16)
            across(c).start()

        for k in range(2):
            pass_on(c, 2, k).wait_recv()
        for k in range(2):
            pass_on(c, 3, k).start()

    def s6(c):
        @pl.when(c != last)
        def _():
            across(c).wait_recv()

            def add(step):
                rows = z_piece(step)
                nd_sum[c, rows, :] = (nd[c, rows, mine].astype(F32) + nd_in[c, rows, :].astype(F32)).astype(BF16)

            add(2)
            far(c).start()
            add(-way)
            near(c).start()
            add(way)
            add(0)

        for k in range(2):
            pass_on(c, 3, k).wait_recv()
        pass_last(c).start()
        for k in (1, 3):
            for d in (1, 2, 3):
                g_x(c, k, d).start()

    def s7(c):
        @pl.when(c != last)
        def _():
            far(c).wait_recv()
            rows = z_piece(way)
            nd_sum[c, rows, :] = (nd_sum[c, rows, :].astype(F32) + far_in[c].astype(F32)).astype(BF16)
            summed(c).start()

        pass_last(c).wait_recv()
        for d in (1, 2, 3):
            g_x(c, 2, d).start()

    def s8(c):
        @pl.when(c == 0)
        def _():
            for copy in over_y:
                copy.wait_recv()

            @pl.loop(0, YS)
            def _(b):
                for k in range(ZH - 1):
                    wide = quarter[b, k].astype(F32)
                    asq_q[k, :, rows_of(b, block)] = (wide * wide).astype(BF16)

        def fisher(k):
            squares = asq_t[z_piece(0), :] if k == 0 else asq_q[k - 1]
            return jnp.dot(squares, gsq[c, (zh + k) % ZH], preferred_element_type=F32)

        for k in (1, 3, 2):
            for d in (1, 2, 3):
                g_x(c, k, d).wait_recv()

        @pl.when(c != last)
        def _():
            total = fisher(0)
            for k in range(1, ZH):
                total = total + fisher(k)
            plain[c] = total
            plain_out[c] = total.astype(BF16)
            across_plain(c).start()

        @pl.when(c == last)
        def _():
            for copy in weights_z:
                copy.wait_recv()
            plain[c] = fisher(0)
            weighted[...] = plain[c] * w[c, z_piece(0), :].astype(F32)
            for k in range(1, ZH):
                one = fisher(k)
                plain[c] += one
                weighted[...] += one * w_early[k - 1].astype(F32)
            plain_out[c] = plain[c].astype(BF16)
            weighted_out[...] = weighted[...].astype(BF16)
            across_plain(c).start()
            across_weighted(c).start()

    def merge(c):
        across_plain(c).wait_recv()
        rows = z_piece(0)
        denom = plain[c, :, mine] + plain_in[c].astype(F32) + 1e-6

        @pl.when(c != last)
        def _():
            near(c).wait_recv()
            summed(c).wait_recv()
            numer = nd_sum[c, rows, :].astype(F32) + near_in[c].astype(F32) + sum_in[c].astype(F32)
            merged[c, rows, mine] = (numer / denom).astype(BF16)

        @pl.when(c == last)
        def _():
            across_weighted(c).wait_recv()
            merged[c, rows, mine] = ((weighted[:, mine] + weighted_in[...].astype(F32)) / denom).astype(BF16)

        spread(c, 0).start()
        spread(c, 1).start()
        share(c, 0).start()

    def s9(c):
        spread(c, 0).wait_recv()
        spread(c, 1).wait_recv()
        forward(c).start()
        share(c, 1).start()
        share(c, 3).start()

    def s10(c):
        forward(c).wait_recv()
        share(c, 2).start()

    def s11(c):
        for step in range(ZH):
            share(c, step).wait_recv()
        store(c).start()
        product(acts, c, merged, part2)
        for d in (1, 2, 3):
            x3(c, d).start()
        sent(c)

        @pl.when(c == 0)
        def _():
            for h in range(2):
                for copy in (up, down, onward):
                    copy[h].wait_send()
            for copy in over_z + over_y + weights_z:
                copy.wait_send()

    def sent(c):
        for d in (1, 2, 3):
            x1(c, d).wait_send()
            x2(c, d).wait_send()
            for k in (1, 2, 3):
                g_x(c, k, d).wait_send()
        for copy in (z1, across_plain, forward, pass_last):
            copy(c).wait_send()
        for k in range(2):
            spread(c, k).wait_send()
            for hop in (1, 2, 3):
                pass_on(c, hop, k).wait_send()

        @pl.when(c != last)
        def _():
            for copy in (across, far, near, summed):
                copy(c).wait_send()

        @pl.when(c == last)
        def _():
            across_weighted(c).wait_send()

        for step in range(ZH):
            share(c, step).wait_send()

    def s12(c):
        for d in (1, 2, 3):
            x3(c, d).wait_recv()
        z_send2[c] = reduce_x(c, part2, part2_in, (1 - zl) * half).astype(BF16)
        z3(c).start()
        row_sum2[c] = reduce_x(c, part2, part2_in, zl * half)

    def s13(c):
        z3(c).wait_recv()
        out[:, pl.ds(pl.multiple_of(c * CW, CW), CW)] = (row_sum2[c] + z_in2[c].astype(F32)).astype(BF16)
        for d in (1, 2, 3):
            x3(c, d).wait_send()
        z3(c).wait_send()
        store(c).wait()

    stages = [s1, s2, s3, s4, s5, s6, s7, s8, merge, s9, s10, s11, s12, s13]

    @pl.loop(0, chunks + len(stages) - 1)
    def _(tick):
        for k in reversed(range(len(stages))):
            c = tick - k

            @pl.when((c >= 0) & (c < chunks))
            def _():
                stages[k](c)


def local(activations, weights, labels, prototypes):
    units = activations.shape[2]
    tok, wide = labels.shape[1], weights.shape[2]
    chunks, block, half, piece = wide // CW, tok // XS, tok // XS // 2, units // ZH

    def vmem(*shape, kind=BF16):
        return pltpu.VMEM(shape, kind)

    anywhere = pl.BlockSpec(memory_space=pl.ANY)
    inside = pl.BlockSpec(memory_space=pltpu.VMEM)
    merged, result = pl.pallas_call(
        functools.partial(kernel, chunks),
        out_shape=(
            jax.ShapeDtypeStruct((units, wide), BF16),
            jax.ShapeDtypeStruct((half, wide), BF16),
        ),
        in_specs=[anywhere] * 4,
        out_specs=(anywhere, inside),
        scratch_shapes=[
            vmem(1, tok, kind=jnp.int32),
            vmem(prototypes.shape[1], wide),
            vmem(YS, units, tok // YS),
            vmem(tok, units),
            vmem(chunks, units, CW),
            vmem(units, tok),
            vmem(block, wide, kind=F32),
            vmem(chunks, tok, CW),
            vmem(chunks, XS - 1, block, CW),
            vmem(chunks, half, CW, kind=F32),
            vmem(chunks, half, CW),
            vmem(chunks, half, CW),
            vmem(chunks, ZH, tok, CW),
            vmem(YS, ZH - 1, piece, tok // YS),
            vmem(ZH - 1, piece, tok),
            vmem(chunks, piece, CW, kind=F32),
            vmem(chunks, piece, CW),
            vmem(chunks, piece, HALF),
            vmem(ZH - 1, piece, CW),
            vmem(piece, CW, kind=F32),
            vmem(piece, CW),
            vmem(piece, HALF),
            vmem(chunks, units, CW),
            vmem(chunks, units, HALF),
            vmem(chunks, units, HALF),
            vmem(chunks, piece, HALF),
            vmem(chunks, piece, HALF),
            vmem(chunks, piece, HALF),
            vmem(chunks, units, CW),
            vmem(chunks, tok, CW),
            vmem(chunks, XS - 1, block, CW),
            vmem(chunks, half, CW, kind=F32),
            vmem(chunks, half, CW),
            vmem(chunks, half, CW),
            pltpu.SemaphoreType.DMA((chunks, SLOTS)),
            pltpu.SemaphoreType.DMA((chunks, SLOTS)),
            pltpu.SemaphoreType.DMA((3, 2)),
            pltpu.SemaphoreType.DMA((3, 2)),
            pltpu.SemaphoreType.DMA((9,)),
            pltpu.SemaphoreType.DMA((9,)),
            pltpu.SemaphoreType.DMA((chunks + 3,)),
            pltpu.SemaphoreType.DMA((chunks,)),
        ],
        compiler_params=pltpu.CompilerParams(
            collective_id=0, has_side_effects=True, vmem_limit_bytes=48 << 20
        ),
    )(activations[0].T, weights[0], labels, prototypes[0])
    return merged, result[None]


def solution(mesh):
    placed = (
        P("task", "col", "row"),
        P("task", "row", "col"),
        P("task", None),
        P("task", None, "col"),
    )
    return jax.shard_map(
        local,
        mesh=mesh,
        in_specs=placed,
        out_specs=(P("row", "col"), P("task", "row", "col")),
        check_vma=False,
    )
```
